256 devices in a mesh: grp: 8 (over x, core), tile: 32 (over y, z).
Axes of the slice: x: 4, y: 4, z: 8, core: 2. Of those that a mesh axis runs over, the one named last changes fastest.
Arguments:
- nodes: bfloat16 [262144, 192], P(('grp', 'tile')), may hold values from -6 to 6
- node_ids: int32 [262144], P(('grp', 'tile')), may hold values from 0 to 262143
- node_count: int32 [256], P(('grp', 'tile')), may hold values from 256 to 1024
- pos_weight: float32 [3, 192], replicated, may hold values from -6 to 6
- gain_one: float32 [192], replicated, may hold values from 0.25 to 1.75
- qkv_one: bfloat16 [192, 576], replicated, may hold values from -0.4375 to 0.4375
- out_one: bfloat16 [192, 192], replicated, may hold values from -0.4375 to 0.4375
- gain_two: float32 [192], replicated, may hold values from 0.25 to 1.75
- qkv_two: bfloat16 [192, 576], replicated, may hold values from -0.4375 to 0.4375
- out_two: bfloat16 [192, 192], replicated, may hold values from -0.4375 to 0.4375
- gain_three: float32 [192], replicated, may hold values from 0.25 to 1.75
- w_up: bfloat16 [192, 768], replicated, may hold values from -0.4375 to 0.4375
- w_down: bfloat16 [768, 192], replicated, may hold values from -0.21875 to 0.21875
- vote_slot: int32 [131072], P(('grp', 'tile')), may hold values from 0 to 1023
- vote_owner: int32 [131072, 1], P(('grp', 'tile')), may hold values from 0 to 31; in each aligned block of 512 rows (0 to 511, 512 to 1023, ...) at most 32 rows name the same one
- vote_voxel: int32 [131072], P(('grp', 'tile')), may hold values from 0 to 255
Outputs:
- features_out: float32 [262144, 192], P(('grp', 'tile'))
- voxel_sums: float32 [65536, 192], P(('grp', 'tile'))
The draws below stay inside these ranges and needn't reach their ends.
Inputs may be any that keep to these rules, and one draw needn't show every extreme that they name: `vote_owner`: among the votes of one shard, at most 32 name any one owner; some owner is named by exactly 32.
All inputs are finite; a program needn't handle non-finite values.
Results may differ from the reference program's by a relative error of at most 0.017.
Values may be sent and summed in bfloat16 or wider, within the bound.
A program may use at most 64 MiB of HBM per device.

```python
import math
import jax
import jax.numpy as jnp
import numpy as np
from jax import lax

C = 192
HEADS = 12
WIN = 32
FF_HID = 768
NODE_DEV = 1024
VOTE_DEV = 512
VOX_DEV = 256
CAP = 32
NODES = 262144
VOTES = 131072
VOXELS = 65536
N_GRP = 8
N_TILE = 32


def place_ends(values, rng, least, high):
    spot = [jax.random.randint(jax.random.fold_in(rng, axis), (), 0, length) for axis, length in enumerate(values.shape)]
    widest = values.shape.index(max(values.shape))
    beside = spot[:widest] + [(spot[widest] + 1) % values.shape[widest]] + spot[widest + 1:]
    return values.at[tuple(spot)].set(least).at[tuple(beside)].set(high)


def steps_of(key, dims, cuts, low, largest):
    def one(dim, parts):
        heights = jax.random.uniform(jax.random.fold_in(jax.random.fold_in(key, 6), dim), (parts,), jnp.float32, low / len(cuts), largest / len(cuts))
        return jnp.repeat(jnp.exp(heights), dims[dim] // parts).reshape((-1,) + (1,) * (len(dims) - dim - 1))

    level = one(*cuts[0])
    for cut in cuts[1:]:
        level = level * one(*cut)
    return level


def routed_block(stream_key, own, number, rows, amount, top, bound, slope):
    order = jax.random.permutation(stream_key, amount)
    packed, common = load_shares(amount, rows * top, bound, slope, True), load_shares(amount, rows * top, bound, slope, False)
    places = jnp.arange(amount)

    def named(sizes, offset_by):
        used = int((sizes > 0).sum())
        fixed = max(1, used // 4)
        moved = fixed + (places - fixed + offset_by * (used - fixed)) % max(1, amount - fixed)
        return jnp.zeros((amount,), jnp.int32).at[order[jnp.where(places < fixed, places, moved)]].set(jnp.asarray(sizes, jnp.int32))

    sizes = jnp.where(number % 4 == 0, named(packed, number // 4), named(common, number - number // 4 - 1))
    mixed = jax.random.permutation(jax.random.fold_in(own, 3), amount)
    source_of, taker = mixed[0:amount // 2 * 2:2], mixed[1:amount // 2 * 2:2]
    slack = jnp.minimum(sizes[source_of] - 1, bound - sizes[taker]) // 2
    slack = jnp.where((source_of == order[0]) | (taker == order[0]) | (sizes[taker] == 0), 0, jnp.maximum(slack, 0))
    moved = jax.random.randint(jax.random.fold_in(own, 4), (amount // 2,), 0, 1 << 20) % (slack + 1)
    sizes = sizes.at[source_of].add(-moved).at[taker].add(moved)
    items = jnp.searchsorted(jnp.cumsum(sizes), jnp.arange(rows * top), side="right").astype(jnp.int32)
    grid = items.reshape(top, rows).T
    grid = grid[jax.random.permutation(jax.random.fold_in(own, 1), rows)]
    offset_by = jax.random.randint(jax.random.fold_in(own, 2), (rows, 1), 0, top)
    return jnp.take_along_axis(grid, (jnp.arange(top)[None, :] + offset_by) % top, axis=1)


def load_shares(number_of, total, most, skew, full):
    portions = [(1 << 20) // math.isqrt(standing ** skew) + 1 for standing in range(1, number_of + 1)]
    largest = most if full else min(most, max(-(-total // number_of), total * portions[0] // sum(portions)))
    least = 1 if total - largest >= number_of - 1 else 0
    given, rest = [largest] + [least] * (number_of - 1), total - largest - least * (number_of - 1)
    while rest > 0:
        movable = [i for i in range(1, number_of) if given[i] < largest] or [i for i in range(1, number_of) if given[i] < most]
        whole, remaining = sum([portions[i] for i in movable]), rest
        for i in movable:
            addition = min(most - given[i], max(1, remaining * portions[i] // whole), rest)
            given[i] = given[i] + addition
            rest = rest - addition
    return np.array(given)


def noise(key, extent, scale, most, cuts=(), kind=jnp.bfloat16):
    values = scale * jax.random.normal(key, extent, jnp.float32)
    if cuts:
        values = values * steps_of(key, extent, cuts, -0.22, 0.18)
    return jnp.clip(values, -most, most).astype(kind)


def setup_inputs(seed: int = 0) -> dict:
    arg_keys = jax.random.split(jax.random.key(seed), 17)
    nodes = noise(arg_keys[0], (NODES, C), 1.0, 6.0, ((0, 256),))
    node_ids = place_ends(jax.random.randint(arg_keys[1], (NODES,), 0, 262144), jax.random.fold_in(arg_keys[1], 1), 0, 262143).astype(jnp.int32)
    node_count = place_ends(jax.random.randint(arg_keys[2], (N_GRP * N_TILE,), NODE_DEV // 4, NODE_DEV + 1), jax.random.fold_in(arg_keys[2], 1), NODE_DEV // 4, NODE_DEV).astype(jnp.int32)
    pos_weight = noise(arg_keys[3], (3, C), 1.0, 6.0, (), jnp.float32)
    gain_one = jnp.clip(1.0 + 0.15 * jax.random.normal(arg_keys[4], (C,), jnp.float32), 0.25, 1.75)
    qkv_one = noise(arg_keys[5], (C, 3 * C), C ** -0.5, 0.4375)
    out_one = noise(arg_keys[6], (C, C), C ** -0.5, 0.4375)
    gain_two = jnp.clip(1.0 + 0.15 * jax.random.normal(arg_keys[7], (C,), jnp.float32), 0.25, 1.75)
    qkv_two = noise(arg_keys[8], (C, 3 * C), C ** -0.5, 0.4375)
    out_two = noise(arg_keys[9], (C, C), C ** -0.5, 0.4375)
    gain_three = jnp.clip(1.0 + 0.15 * jax.random.normal(arg_keys[10], (C,), jnp.float32), 0.25, 1.75)
    w_up = noise(arg_keys[11], (C, FF_HID), C ** -0.5, 0.4375)
    w_down = noise(arg_keys[12], (FF_HID, C), FF_HID ** -0.5, 0.21875)
    vote_slot = place_ends(jax.random.randint(arg_keys[13], (VOTES,), 0, NODE_DEV), jax.random.fold_in(arg_keys[13], 1), 0, NODE_DEV - 1).astype(jnp.int32)
    vote_owner_keys = jax.random.split(jax.random.fold_in(arg_keys[14], 1), VOTES // VOTE_DEV)
    vote_owner_turns = jax.random.permutation(jax.random.fold_in(arg_keys[14], 3), VOTES // VOTE_DEV)
    vote_owner = jax.vmap(lambda own, number: routed_block(jax.random.fold_in(arg_keys[14], 2), own, number, VOTE_DEV, N_TILE, 1, CAP, 2))(vote_owner_keys, vote_owner_turns).reshape((VOTES, 1))
    vote_voxel = place_ends(jax.random.randint(arg_keys[15], (VOTES,), 0, VOX_DEV), jax.random.fold_in(arg_keys[15], 1), 0, VOX_DEV - 1).astype(jnp.int32)
    return {"nodes": nodes, "node_ids": node_ids, "node_count": node_count, "pos_weight": pos_weight, "gain_one": gain_one, "qkv_one": qkv_one, "out_one": out_one, "gain_two": gain_two, "qkv_two": qkv_two, "out_two": out_two, "gain_three": gain_three, "w_up": w_up, "w_down": w_down, "vote_slot": vote_slot, "vote_owner": vote_owner, "vote_voxel": vote_voxel}


def position(node_ids, pos_weight):
    rows = []
    for axis in range(3):
        total = jnp.zeros(node_ids.shape, jnp.int32)
        for level in range(6):
            bit = jnp.bitwise_and(jnp.right_shift(node_ids, 3 * level + axis), 1)
            total = total + bit * 2 ** level
        rows.append(total.astype(jnp.float32) / 64.0 - 0.5)
    coords = jnp.stack(rows, 0)
    return jnp.einsum('an,ac->nc', coords, pos_weight, precision=lax.Precision.HIGHEST)

def normed(x, gain):
    mean = lax.optimization_barrier(jnp.mean(x, -1, keepdims=True))
    var = lax.optimization_barrier(jnp.mean((x - mean) ** 2, -1, keepdims=True))
    return ((x - mean) * lax.rsqrt(var + 1e-05) * gain).astype(jnp.bfloat16)

def attend(windows, keep, gain, w_qkv, w_out):
    xf = windows.astype(jnp.float32)
    count, width, chans = windows.shape
    head_dim = chans // HEADS
    inner = normed(xf, gain)
    qkv = jnp.einsum('nwc,cd->nwd', inner.astype(jnp.float32), w_qkv.astype(jnp.float32)).astype(jnp.bfloat16)
    qkv = qkv.reshape(count, width, 3, HEADS, head_dim).astype(jnp.float32)
    query, keys, values = (qkv[:, :, 0], qkv[:, :, 1], qkv[:, :, 2])
    scores = jnp.einsum('nqhd,nkhd->nhqk', query, keys) * head_dim ** (-0.5)
    scores = scores + ((keep - 1.0) * 1000000000.0)[:, None, None, :]
    probs = jax.nn.softmax(scores, -1).astype(jnp.bfloat16)
    context = jnp.einsum('nhqk,nkhd->nqhd', probs.astype(jnp.float32), values).reshape(count, width, chans)
    context = context.astype(jnp.bfloat16)
    return xf + jnp.einsum('nwc,cd->nwd', context.astype(jnp.float32), w_out.astype(jnp.float32))

def feed(x, gain, w_up, w_down):
    inner = normed(x, gain)
    hidden = jax.nn.gelu(jnp.einsum('nwc,cd->nwd', inner.astype(jnp.float32), w_up.astype(jnp.float32))).astype(jnp.bfloat16)
    return x + jnp.einsum('nwd,dc->nwc', hidden.astype(jnp.float32), w_down.astype(jnp.float32))

def reference(nodes, node_ids, node_count, pos_weight, gain_one, qkv_one, out_one, gain_two, qkv_two, out_two, gain_three, w_up, w_down, vote_slot, vote_owner, vote_voxel):
    shards = N_GRP * N_TILE
    block = NODE_DEV // N_GRP
    run = WIN // N_GRP
    keep = (jnp.arange(NODE_DEV, dtype=jnp.int32)[None, :] < node_count[:, None]).astype(jnp.float32).reshape(-1)
    start = (nodes.astype(jnp.float32) + position(node_ids, pos_weight)).astype(jnp.bfloat16)

    def local(pair):
        return attend(pair[0], pair[1], gain_one, qkv_one, out_one).astype(jnp.bfloat16)
    first = lax.map(local, (start.reshape(shards, NODE_DEV // WIN, WIN, C), keep.reshape(shards, NODE_DEV // WIN, WIN)))

    def arrange(array):
        shaped = array.reshape(N_GRP, N_TILE, N_GRP, block // run, run, -1)
        return shaped.transpose(1, 2, 3, 0, 4, 5).reshape(N_TILE, N_GRP * (block // run), WIN, -1)

    def dilated(pair):
        mixed = attend(pair[0], pair[1][..., 0], gain_two, qkv_two, out_two)
        return feed(mixed, gain_three, w_up, w_down)
    third = lax.map(dilated, (arrange(first), arrange(keep[:, None])))
    third = third.reshape(N_TILE, N_GRP, block // run, N_GRP, run, C).transpose(3, 0, 1, 2, 4, 5).reshape(NODES, C)
    features_out = third.astype(jnp.float32) * keep[:, None]
    index = jnp.arange(VOTES, dtype=jnp.int32)
    shard = index // VOTE_DEV
    global_node = shard * NODE_DEV + vote_slot
    group = shard // N_TILE
    voxel = (group * N_TILE + vote_owner[:, 0]) * VOX_DEV + vote_voxel
    picked = features_out[global_node].astype(jnp.bfloat16).astype(jnp.float32)
    voxel_sums = jax.ops.segment_sum(picked, voxel, num_segments=VOXELS)
    return (features_out, voxel_sums)
```

```python
import jax
import jax.numpy as jnp
from jax import lax
from jax.sharding import PartitionSpec as P

HEADS = 12
WIN = 32
VOX_DEV = 256
CAP = 32


def position(node_ids, pos_weight):
    rows = []
    for axis in range(3):
        total = jnp.zeros(node_ids.shape, jnp.int32)
        for level in range(6):
            bit = jnp.bitwise_and(jnp.right_shift(node_ids, 3 * level + axis), 1)
            total = total + bit * 2**level
        rows.append(total.astype(jnp.float32) / 64.0 - 0.5)
    coords = jnp.stack(rows, 0)
    return jnp.einsum("an,ac->nc", coords, pos_weight, precision=lax.Precision.HIGHEST)


def normed(x, gain):
    mean = jnp.mean(x, -1, keepdims=True)
    var = jnp.mean((x - mean) ** 2, -1, keepdims=True)
    return ((x - mean) * lax.rsqrt(var + 1e-05) * gain).astype(jnp.bfloat16)


def attend(windows, keep, gain, w_qkv, w_out):
    xf = windows.astype(jnp.float32)
    count, width, chans = windows.shape
    head_dim = chans // HEADS
    inner = normed(xf, gain)
    qkv = jnp.einsum("nwc,cd->nwd", inner, w_qkv, preferred_element_type=jnp.float32).astype(
        jnp.bfloat16
    )
    qkv = qkv.reshape(count, width, 3, HEADS, head_dim)
    query, keys, values = (qkv[:, :, 0], qkv[:, :, 1], qkv[:, :, 2])
    scores = jnp.einsum(
        "nqhd,nkhd->nhqk", query, keys, preferred_element_type=jnp.float32
    ) * head_dim ** (-0.5)
    scores = scores + ((keep - 1.0) * 1000000000.0)[:, None, None, :]
    probs = jax.nn.softmax(scores, -1).astype(jnp.bfloat16)
    context = jnp.einsum("nhqk,nkhd->nqhd", probs, values, preferred_element_type=jnp.float32)
    context = context.reshape(count, width, chans).astype(jnp.bfloat16)
    return xf + jnp.einsum("nwc,cd->nwd", context, w_out, preferred_element_type=jnp.float32)


def feed(x, gain, w_up, w_down):
    inner = normed(x, gain)
    hidden = jax.nn.gelu(
        jnp.einsum("nwc,cd->nwd", inner, w_up, preferred_element_type=jnp.float32)
    ).astype(jnp.bfloat16)
    return x + jnp.einsum("nwd,dc->nwc", hidden, w_down, preferred_element_type=jnp.float32)


def pack_votes(owner, voxel):
    tiles = lax.axis_size("tile")
    votes = owner.shape[0]
    named = (owner[:, None] == jnp.arange(tiles, dtype=jnp.int32)[None, :]).astype(jnp.bfloat16)
    index = jnp.arange(votes, dtype=jnp.int32)
    earlier = (index[None, :] < index[:, None]).astype(jnp.bfloat16)
    rank = jnp.sum(jnp.dot(earlier, named, preferred_element_type=jnp.float32) * named, 1)
    place = owner * CAP + rank.astype(jnp.int32)
    packing = (jnp.arange(tiles * CAP, dtype=jnp.int32)[:, None] == place[None, :]).astype(jnp.bfloat16)
    voxels = jnp.dot(packing, voxel.astype(jnp.bfloat16)[:, None], preferred_element_type=jnp.float32)
    received = lax.all_to_all(
        voxels.astype(jnp.bfloat16).reshape(tiles, CAP), "tile", split_axis=0, concat_axis=0, tiled=True
    )
    return packing, received.reshape(tiles * CAP).astype(jnp.int32)


def body(
    nodes,
    node_ids,
    node_count,
    pos_weight,
    gain_one,
    qkv_one,
    out_one,
    gain_two,
    qkv_two,
    out_two,
    gain_three,
    w_up,
    w_down,
    vote_slot,
    vote_owner,
    vote_voxel,
):
    n_local, width = nodes.shape
    packing, voxel_of = pack_votes(vote_owner[:, 0], vote_voxel)
    groups = lax.axis_size("grp")
    block = n_local // groups
    run = WIN // groups
    keep = (jnp.arange(n_local, dtype=jnp.int32) < node_count[0]).astype(jnp.float32)
    start = (nodes.astype(jnp.float32) + position(node_ids, pos_weight)).astype(jnp.bfloat16)
    first = attend(
        start.reshape(n_local // WIN, WIN, width),
        keep.reshape(n_local // WIN, WIN),
        gain_one,
        qkv_one,
        out_one,
    )
    first = first.astype(jnp.bfloat16).reshape(groups, block, width)
    arrived, arrived_keep = (
        lax.all_to_all(first, "grp", split_axis=0, concat_axis=0, tiled=True),
        lax.all_to_all(
            keep.astype(jnp.bfloat16).reshape(groups, block),
            "grp",
            split_axis=0,
            concat_axis=0,
            tiled=True,
        ),
    )
    windows = (
        arrived.reshape(groups, block // run, run, width)
        .transpose(1, 0, 2, 3)
        .reshape(block // run, WIN, width)
    )
    window_keep = (
        arrived_keep.reshape(groups, block // run, run)
        .transpose(1, 0, 2)
        .reshape(block // run, WIN)
    )
    second = attend(windows, window_keep.astype(jnp.float32), gain_two, qkv_two, out_two)
    third = feed(second, gain_three, w_up, w_down)
    outgoing = (
        third.reshape(block // run, groups, run, width)
        .transpose(1, 0, 2, 3)
        .reshape(groups, block, width)
    )
    returned = (
        lax.all_to_all(
            outgoing.astype(jnp.bfloat16), "grp", split_axis=0, concat_axis=0, tiled=True
        )
        .astype(outgoing.dtype)
        .reshape(n_local, width)
    )
    features_out = returned * keep[:, None]
    tiles = lax.axis_size("tile")
    received = lax.all_to_all(
        jnp.dot(packing, features_out.astype(jnp.bfloat16)[vote_slot], preferred_element_type=jnp.float32)
        .astype(jnp.bfloat16)
        .reshape(tiles, CAP, width),
        "tile",
        split_axis=0,
        concat_axis=0,
        tiled=True,
    ).reshape(tiles * CAP, width)
    sums = (jnp.arange(VOX_DEV, dtype=jnp.int32)[:, None] == voxel_of[None, :]).astype(jnp.bfloat16)
    voxel_sums = jnp.dot(sums, received, preferred_element_type=jnp.float32)
    return (features_out, voxel_sums)


def solution(mesh):
    in_specs = (
        P(("grp", "tile"), None),
        P(("grp", "tile")),
        P(("grp", "tile")),
        P(),
        P(),
        P(),
        P(),
        P(),
        P(),
        P(),
        P(),
        P(),
        P(),
        P(("grp", "tile")),
        P(("grp", "tile"), None),
        P(("grp", "tile")),
    )
    out_specs = (P(("grp", "tile"), None), P(("grp", "tile"), None))
    return jax.shard_map(body, mesh=mesh, in_specs=in_specs, out_specs=out_specs, check_vma=False)
```

```python
import functools
import jax
import jax.numpy as jnp
from jax import lax
from jax.experimental import pallas as pl
from jax.experimental.pallas import tpu as pltpu
from jax.sharding import PartitionSpec as P

HEADS = 12
WIN = 32
VOX_DEV = 256
CAP = 32
LANES = 128
F32 = jnp.float32
BF16 = jnp.bfloat16
NT = (((1,), (1,)), ((), ()))
TN = (((0,), (0,)), ((), ()))
MESH = pl.DeviceIdType.MESH


def iota(shape, dim):
    return lax.broadcasted_iota(jnp.int32, shape, dim)


def mm(a, b, dims=(((1,), (0,)), ((), ()))):
    return lax.dot_general(a, b, dims, preferred_element_type=F32)


def normed(x, gain):
    mean = jnp.mean(x, -1, keepdims=True)
    var = jnp.mean((x - mean) ** 2, -1, keepdims=True)
    return ((x - mean) * lax.rsqrt(var + 1e-05) * gain).astype(BF16)


def attend(x, biases, gain, w_qv, w_k, w_out):
    chans = x.shape[1]
    dim = chans // HEADS
    inner = normed(x, gain)
    qv = mm(w_qv, inner, NT).astype(BF16)
    keys = mm(inner, w_k).astype(BF16)
    lane_win = iota((WIN, LANES), 1) // WIN
    own = [lane_win == w for w in range(LANES // WIN)]
    zero = jnp.zeros((WIN, LANES), BF16)
    halves = []
    for half, bias in enumerate(biases):
        lanes = slice(LANES * half, LANES * half + LANES)
        context = []
        for first in range(0, HEADS, 2):
            part = first * dim // LANES * LANES
            depth = min(LANES, chans - part)
            blocks = []
            for head in (first, first + 1):
                above = head * dim - part
                below = depth - above - dim
                pieces = [qv[head * dim : head * dim + dim, lanes]]
                if above:
                    pieces.insert(0, jnp.zeros((above, LANES), BF16))
                if below:
                    pieces.append(jnp.zeros((below, LANES), BF16))
                blocks.append(jnp.concatenate(pieces, 0))
            full = mm(keys[lanes, part : part + depth], jnp.concatenate(blocks, 1))
            probs, totals = [], []
            for i in range(2):
                wide = full[:, LANES * i : LANES * i + LANES]
                scores = wide[:WIN]
                for w in range(1, LANES // WIN):
                    scores = jnp.where(own[w], wide[WIN * w : WIN * w + WIN], scores)
                scores = scores + bias
                weights = jnp.exp(scores - jnp.max(scores, 0, keepdims=True))
                totals.append(jnp.sum(weights, 0, keepdims=True))
                weights = weights.astype(BF16)
                probs.append(jnp.concatenate([jnp.where(m, weights, zero) for m in own], 0))
            values = qv[chans + first * dim : chans + (first + 2) * dim, lanes]
            mixed = mm(values, jnp.concatenate(probs, 1))
            for i in range(2):
                piece = mixed[dim * i : dim * i + dim, LANES * i : LANES * i + LANES]
                context.append((piece / totals[i]).astype(BF16))
        halves.append(jnp.concatenate(context, 0))
    return x + mm(jnp.concatenate(halves, 1), w_out, TN)


def feed(x, gain, w_up, w_down):
    up = mm(normed(x, gain), w_up)
    inside = up * (0.7978845608028654 + 0.035677408136300125 * up * up)
    hidden = (0.5 * up * (1.0 + jnp.tanh(inside))).astype(BF16)
    return x + mm(hidden, w_down)


def turned(w, chans):
    dim = chans // HEADS
    eye = (iota((chans, chans), 0) == iota((chans, chans), 1)).astype(BF16)
    query = (mm(eye, w[:, :chans], NT) * dim**-0.5).astype(BF16)
    value = mm(eye, w[:, 2 * chans :], NT).astype(BF16)
    return jnp.concatenate([query, value], 0)


def columns(row):
    parts = []
    for t in range(row.shape[1] // LANES):
        piece = row[:, LANES * t : LANES * t + LANES].astype(F32)
        parts.append(jnp.broadcast_to(piece, (LANES, LANES)).T)
    return jnp.concatenate(parts, 0)


def place_positions(start, nodes, ids, pos_weight):
    groups, chunks, win, chans = start.shape
    row = iota((16, chans), 0)
    pick = [pos_weight[a : a + 1, :] for a in range(3)]
    spread = jnp.where(row % 3 == 0, pick[0], jnp.where(row % 3 == 1, pick[1], pick[2]))
    high = spread.astype(BF16).astype(F32)
    middle = (spread - high).astype(BF16).astype(F32)
    low = spread - high - middle
    split = jnp.where(row < 3, high, jnp.where(row < 6, middle, jnp.where(row < 9, low, 0.0))).astype(BF16)
    axes = []
    for axis in range(3):
        total = jnp.zeros(ids.shape, jnp.int32)
        for level in range(6):
            total = total + jnp.bitwise_and(jnp.right_shift(ids, 3 * level + axis), 1) * 2**level
        axes.append(total.astype(F32) / 64.0 - 0.5)
    slim = iota((16, LANES), 0)
    for g in range(groups):
        line = [a[g : g + 1, :] for a in axes]
        coords = jnp.where(slim % 3 == 0, line[0], jnp.where(slim % 3 == 1, line[1], line[2])).astype(BF16)
        moved = nodes[LANES * g : LANES * g + LANES, :].astype(F32) + mm(coords, split, TN)
        start[g] = moved.astype(BF16).reshape(chunks, win, chans)


def kernel(
    count_ref, nodes, ids, pos_weight, gain_one, qkv_one, out_one, gain_two, qkv_two, out_two,
    gain_three, w_up, w_down, slot_ref, owner_ref, voxel_ref,
    feat_out, vox_out,
    start, qv_one, qv_two, sent_one, got_one, sent_two, got_two, count_sent, count_got,
    vox_sent, vox_got, votes_sent, votes_got,
    count_ss, count_rs, vox_ss, vox_rs, one_ss, one_rs, two_ss, two_rs, vote_ss, vote_rs,
    *, groups, tiles,
):
    me, tile = lax.axis_index("grp"), lax.axis_index("tile")
    chans = nodes.shape[1]
    chunks = start.shape[1]
    block = chunks * WIN
    run = WIN // groups
    rows = groups * WIN
    count = count_ref[0]

    barrier = pltpu.get_barrier_semaphore()
    for d in range(1, groups):
        pl.semaphore_signal(barrier, inc=1, device_id=(lax.rem(me + d, groups), tile), device_id_type=MESH)
    for d in range(1, tiles):
        pl.semaphore_signal(barrier, inc=1, device_id=(me, lax.rem(tile + d, tiles)), device_id_type=MESH)

    def to_group(d, src, dst, ss, rs):
        return pltpu.make_async_remote_copy(
            src_ref=src, dst_ref=dst, send_sem=ss, recv_sem=rs,
            device_id=(lax.rem(me + d, groups), tile), device_id_type=MESH,
        )

    def to_tile(d, src, dst, ss, rs):
        return pltpu.make_async_remote_copy(
            src_ref=src, dst_ref=dst, send_sem=ss, recv_sem=rs,
            device_id=(me, lax.rem(tile + d, tiles)), device_id_type=MESH,
        )

    def count_copy(d):
        return to_group(d, count_sent, count_got.at[me], count_ss.at[d], count_rs.at[d])

    def vox_copy(d):
        peer = lax.rem(tile + d, tiles)
        return to_tile(d, vox_sent.at[peer], vox_got.at[tile], vox_ss.at[d], vox_rs.at[d])

    def one_copy(d, c):
        peer = lax.rem(me + d, groups)
        return to_group(d, sent_one.at[c, peer], got_one.at[c, me], one_ss.at[c, d], one_rs.at[c, d])

    def two_copy(d, c):
        peer = lax.rem(me + d, groups)
        return to_group(d, sent_two.at[c, peer], got_two.at[me, c], two_ss.at[c, d], two_rs.at[c, d])

    def vote_copy(d):
        peer = lax.rem(tile + d, tiles)
        return to_tile(d, votes_sent.at[peer], votes_got.at[tile], vote_ss.at[d], vote_rs.at[d])

    count_sent[...] = jnp.full(count_sent.shape, count, jnp.int32)
    count_got[me] = jnp.full(count_sent.shape, count, jnp.int32)
    place_positions(start, nodes, ids[...], pos_weight[...])
    qv_one[...] = turned(qkv_one[...], chans)
    qv_two[...] = turned(qkv_two[...], chans)

    votes = owner_ref.shape[1]
    owner = owner_ref[...].astype(F32)
    owner_col = columns(owner)
    earlier, later = iota((votes, LANES), 0), iota((votes, LANES), 1)
    ranks = []
    for t in range(votes // LANES):
        same = jnp.logical_and(owner_col == owner[:, LANES * t : LANES * t + LANES], earlier < later + LANES * t)
        ranks.append(jnp.sum(jnp.where(same, 1.0, 0.0), 0, keepdims=True))
    rank = jnp.concatenate(ranks, 1)
    place = owner * CAP + rank
    named = jnp.where(iota((tiles, votes), 0).astype(F32) == owner, voxel_ref[...].astype(F32), 0.0).astype(BF16)
    lane = iota((votes, LANES), 1)
    ranked = (columns(rank) == (lane % CAP).astype(F32)).astype(BF16)
    table = mm(named, ranked)
    share = LANES // CAP
    table = jnp.where(iota((tiles, LANES), 1) // CAP == lax.rem(tile, share), table, 0.0)
    for t in range(tiles):
        vox_sent[t] = jnp.broadcast_to(table[t : t + 1, :], vox_sent.shape[1:])
    vox_got[tile] = vox_sent[tile]

    pl.semaphore_wait(barrier, groups + tiles - 2)
    for d in range(1, groups):
        count_copy(d).start()
    for d in range(1, tiles):
        vox_copy(d).start()

    key = iota((WIN, LANES), 0)
    window = iota((WIN, LANES), 1) // WIN

    def stage_one(c, carry):
        x = jnp.concatenate([start[g, c] for g in range(groups)], 0).astype(F32)
        biases = []
        for half in range(rows // LANES):
            slot = (window + half * (LANES // WIN)) * block + c * WIN + key
            kept = jnp.where(slot < count, 1.0, 0.0)
            biases.append((kept - 1.0) * 1000000000.0)
        first = attend(x, biases, gain_one[...], qv_one[...], qkv_one[:, chans : 2 * chans], out_one[...])
        sent_one[c] = first.astype(BF16).reshape(groups, WIN, chans)
        got_one[c, me] = sent_one[c, me]
        for d in range(1, groups):
            one_copy(d, c).start()
        return carry

    lax.fori_loop(0, chunks, stage_one, 0)

    for d in range(1, groups):
        count_copy(d).wait_recv()
    counts = jnp.zeros((WIN, LANES), jnp.int32)
    for g in range(groups):
        counts = jnp.where(key // run == g, count_got[g][:1, :], counts)
    swap = (
        iota((rows, rows), 1)
        == iota((rows, rows), 0) // run % groups * WIN + iota((rows, rows), 0) // WIN * run + iota((rows, rows), 0) % run
    ).astype(BF16)

    def stage_two(c, carry):
        for d in range(1, groups):
            one_copy(d, c).wait_recv()
        x = mm(swap, got_one[c].reshape(rows, chans))
        biases = []
        for half in range(rows // LANES):
            slot = me * block + c * WIN + (half * (LANES // WIN) + window) * run + key % run
            kept = jnp.where(slot < counts, 1.0, 0.0)
            biases.append((kept - 1.0) * 1000000000.0)
        second = attend(x, biases, gain_two[...], qv_two[...], qkv_two[:, chans : 2 * chans], out_two[...])
        third = feed(second, gain_three[...], w_up[...], w_down[...])
        sent_two[c] = mm(swap, third.astype(BF16)).astype(BF16).reshape(groups, WIN, chans)
        got_two[me, c] = sent_two[c, me]
        for d in range(1, groups):
            two_copy(d, c).start()
        return carry

    lax.fori_loop(0, chunks, stage_two, 0)

    slots = nodes.shape[0]
    slot_col = columns(slot_ref[...])
    chosen = jnp.concatenate(
        [(slot_col == (lane + LANES * t).astype(F32)).astype(BF16) for t in range(slots // LANES)], 1
    )
    for d in range(1, tiles):
        vox_copy(d).wait_recv()
    vox = iota((VOX_DEV, LANES), 0).astype(F32)
    sums = []
    for a in range(tiles // share):
        mine = vox_got[share * a]
        for u in range(1, share):
            mine = mine + vox_got[share * a + u]
        sums.append((vox == mine[:1, :]).astype(BF16))
    sums = jnp.concatenate(sums, 1)

    for c in range(chunks):
        for d in range(1, groups):
            two_copy(d, c).wait_recv()
    back = got_two[...].reshape(slots, chans)
    feat = jnp.where(iota((slots, chans), 0) < count, back.astype(F32), 0.0).astype(BF16)
    feat_out[...] = feat
    picked = mm(chosen, feat).astype(BF16)
    packing = (iota((tiles * CAP, votes), 0).astype(F32) == place).astype(BF16)
    votes_sent[...] = mm(packing, picked).astype(BF16).reshape(tiles, CAP, chans)
    votes_got[tile] = votes_sent[tile]
    for d in range(1, tiles):
        vote_copy(d).start()
    for d in range(1, tiles):
        vote_copy(d).wait_recv()
    vox_out[...] = mm(sums, votes_got[...].reshape(tiles * CAP, chans))

    for d in range(1, groups):
        count_copy(d).wait_send()
        for c in range(chunks):
            one_copy(d, c).wait_send()
            two_copy(d, c).wait_send()
    for d in range(1, tiles):
        vox_copy(d).wait_send()
        vote_copy(d).wait_send()


def body(
    nodes, node_ids, node_count, pos_weight, gain_one, qkv_one, out_one, gain_two, qkv_two, out_two,
    gain_three, w_up, w_down, vote_slot, vote_owner, vote_voxel,
):
    slots, chans = nodes.shape
    votes = vote_slot.shape[0]
    groups, tiles = lax.axis_size("grp"), lax.axis_size("tile")
    chunks = slots // groups // WIN
    vmem = pl.BlockSpec(memory_space=pltpu.VMEM)
    dma = pltpu.SemaphoreType.DMA


    feat, sums = pl.pallas_call(
        functools.partial(kernel, groups=groups, tiles=tiles),
        out_shape=(
            jax.ShapeDtypeStruct((slots, chans), BF16),
            jax.ShapeDtypeStruct((VOX_DEV, chans), F32),
        ),
        in_specs=[pl.BlockSpec(memory_space=pltpu.SMEM)] + [vmem] * 15,
        out_specs=(vmem, vmem),
        scratch_shapes=[
            pltpu.VMEM((groups, chunks, WIN, chans), BF16),
            pltpu.VMEM((2 * chans, chans), BF16),
            pltpu.VMEM((2 * chans, chans), BF16),
            pltpu.VMEM((chunks, groups, WIN, chans), BF16),
            pltpu.VMEM((chunks, groups, WIN, chans), BF16),
            pltpu.VMEM((chunks, groups, WIN, chans), BF16),
            pltpu.VMEM((groups, chunks, WIN, chans), BF16),
            pltpu.VMEM((8, LANES), jnp.int32),
            pltpu.VMEM((groups, 8, LANES), jnp.int32),
            pltpu.VMEM((tiles, 8, LANES), F32),
            pltpu.VMEM((tiles, 8, LANES), F32),
            pltpu.VMEM((tiles, CAP, chans), BF16),
            pltpu.VMEM((tiles, CAP, chans), BF16),
            dma((groups,)), dma((groups,)), dma((tiles,)), dma((tiles,)),
            dma((chunks, groups)), dma((chunks, groups)), dma((chunks, groups)), dma((chunks, groups)),
            dma((tiles,)), dma((tiles,)),
        ],
        compiler_params=pltpu.CompilerParams(collective_id=0, has_side_effects=True),
    )(
        node_count, nodes, node_ids.reshape(slots // LANES, LANES), pos_weight,
        gain_one.reshape(1, chans), qkv_one, out_one, gain_two.reshape(1, chans), qkv_two, out_two,
        gain_three.reshape(1, chans), w_up, w_down,
        vote_slot.reshape(1, votes), vote_owner.reshape(1, votes), vote_voxel.reshape(1, votes),
    )
    return feat.astype(F32), sums


def solution(mesh):
    in_specs = (
        P(("grp", "tile"), None),
        P(("grp", "tile")),
        P(("grp", "tile")),
        P(),
        P(),
        P(),
        P(),
        P(),
        P(),
        P(),
        P(),
        P(),
        P(),
        P(("grp", "tile")),
        P(("grp", "tile"), None),
        P(("grp", "tile")),
    )
    out_specs = (P(("grp", "tile"), None), P(("grp", "tile"), None))
    return jax.shard_map(body, mesh=mesh, in_specs=in_specs, out_specs=out_specs, check_vma=False)
```

```python
import functools
import jax
import jax.numpy as jnp
from jax import lax
from jax.experimental import pallas as pl
from jax.experimental.pallas import tpu as pltpu
from jax.sharding import PartitionSpec as P

HEADS = 12
WIN = 32
VOX_DEV = 256
CAP = 32
LANES = 128
F32 = jnp.float32
BF16 = jnp.bfloat16
NT = (((1,), (1,)), ((), ()))
TN = (((0,), (0,)), ((), ()))
MESH = pl.DeviceIdType.MESH
LOG2E = 1.4426950408889634


def iota(shape, dim):
    return lax.broadcasted_iota(jnp.int32, shape, dim)


def mm(a, b, dims=(((1,), (0,)), ((), ()))):
    return lax.dot_general(a, b, dims, preferred_element_type=F32)


def normed(x, gain):
    mean = jnp.mean(x, 0, keepdims=True)
    var = jnp.mean((x - mean) ** 2, 0, keepdims=True)
    return ((x - mean) * lax.rsqrt(var + 1e-05) * jnp.concatenate([gain] * (x.shape[1] // LANES), 1)).astype(BF16)


def attend(x, biases, gain, w_qkv, w_out):
    chans = x.shape[0]
    dim = chans // HEADS
    wins = LANES // WIN
    qkv = mm(w_qkv, normed(x, gain))
    query = (qkv[:chans] * (dim**-0.5 * LOG2E)).astype(BF16)
    keys = qkv[chans : 2 * chans].astype(BF16)
    values = qkv[2 * chans :].astype(BF16)
    lane_win = iota((WIN, LANES), 1) // WIN
    own = [lane_win == w for w in range(wins)]
    own_short = [m[:dim] for m in own]
    zero = jnp.zeros((dim, LANES), BF16)
    pairs = [(half, first) for half in range(len(biases)) for first in range(0, HEADS, 2)]
    scores = {}
    for half, first in pairs:
        lanes = slice(LANES * half, LANES * half + LANES)
        rows = slice(first * dim, first * dim + 2 * dim)
        two = query[rows, lanes]
        blocks = jnp.concatenate(
            [jnp.concatenate([two[:dim], zero], 1), jnp.concatenate([zero, two[dim:]], 1)], 0
        )
        full = mm(keys[rows, lanes], blocks, TN)
        for i in range(2):
            wide = full[:, LANES * i : LANES * i + LANES]
            picked = wide[:WIN]
            for w in range(1, wins):
                picked = jnp.where(own[w], wide[WIN * w : WIN * w + WIN], picked)
            scores[half, first + i] = picked + biases[half]
    probs, totals = {}, {}
    for key, score in scores.items():
        weights = jnp.exp2(score - jnp.max(score, 0, keepdims=True))
        totals[key] = 1.0 / jnp.sum(weights, 0, keepdims=True)
        probs[key] = weights.astype(BF16)
    context = {}
    for half, first in pairs:
        rows = slice(first * dim, first * dim + 2 * dim)
        stacked = jnp.concatenate(
            [values[rows, LANES * half + WIN * w : LANES * half + WIN * w + WIN] for w in range(wins)], 0
        )
        mixed = mm(stacked, jnp.concatenate([probs[half, first], probs[half, first + 1]], 1))
        for i in range(2):
            wide = mixed[:, LANES * i : LANES * i + LANES]
            at = [2 * dim * w + dim * i for w in range(wins)]
            picked = wide[at[0] : at[0] + dim]
            for w in range(1, wins):
                picked = jnp.where(own_short[w], wide[at[w] : at[w] + dim], picked)
            context[half, first + i] = (picked * totals[half, first + i]).astype(BF16)
    merged = jnp.concatenate(
        [jnp.concatenate([context[half, h] for h in range(HEADS)], 0) for half in range(len(biases))], 1
    )
    return x + mm(w_out, merged)


def feed(x, gain, w_up, w_down):
    up = mm(w_up, normed(x, gain))
    inside = up * (0.7978845608028654 + 0.035677408136300125 * up * up)
    hidden = (0.5 * up * (1.0 + jnp.tanh(inside))).astype(BF16)
    return x + mm(w_down, hidden)


def swapped(x, groups):
    half = x.shape[0] // groups // 2
    run = WIN // groups
    parts = x.reshape(groups // 2, 2, groups // 2, 2 * run, x.shape[1])
    low = iota((2 * run, x.shape[1]), 0) < run
    out = []
    for b in range(groups // 2):
        for odd in range(2):
            for a in range(groups // 2):
                first, second = parts[a, 0, b], parts[a, 1, b]
                if odd:
                    out.append(jnp.where(low, pltpu.roll(first, run, 0), second))
                else:
                    out.append(jnp.where(low, first, pltpu.roll(second, run, 0)))
    return jnp.concatenate(out, 0)


def turned(w):
    return w.astype(F32).T.astype(BF16)


def columns(row):
    parts = []
    for t in range(row.shape[1] // LANES):
        piece = row[:, LANES * t : LANES * t + LANES].astype(F32)
        parts.append(jnp.broadcast_to(piece, (LANES, LANES)).T)
    return jnp.concatenate(parts, 0)


def place_positions(start, nodes, ids, pos_weight):
    groups, chunks, win, chans = start.shape
    row = iota((16, chans), 0)
    pick = [pos_weight[a : a + 1, :] for a in range(3)]
    spread = jnp.where(row % 3 == 0, pick[0], jnp.where(row % 3 == 1, pick[1], pick[2]))
    high = spread.astype(BF16).astype(F32)
    middle = (spread - high).astype(BF16).astype(F32)
    low = spread - high - middle
    split = jnp.where(row < 3, high, jnp.where(row < 6, middle, jnp.where(row < 9, low, 0.0))).astype(BF16)
    axes = []
    for axis in range(3):
        total = jnp.zeros(ids.shape, jnp.int32)
        for level in range(6):
            total = total + jnp.bitwise_and(jnp.right_shift(ids, 3 * level + axis), 1) * 2**level
        axes.append(total.astype(F32) / 64.0 - 0.5)
    slim = iota((16, LANES), 0)
    for g in range(groups):
        line = [a[g : g + 1, :] for a in axes]
        coords = jnp.where(slim % 3 == 0, line[0], jnp.where(slim % 3 == 1, line[1], line[2])).astype(BF16)
        moved = nodes[:, LANES * g : LANES * g + LANES].astype(F32) + mm(split, coords, TN)
        start[g] = moved.T.astype(BF16).reshape(chunks, win, chans)


def kernel(
    count_ref, nodes, ids, pos_weight, gain_one, qkv_one, out_one, gain_two, qkv_two, out_two,
    gain_three, w_up, w_down, slot_ref, owner_ref, voxel_ref,
    feat_out, vox_out,
    start, in_one, proj_one, in_two, proj_two, up_turned, norm_one, norm_two, norm_three, sent_one, got_one, sent_two, got_two, count_sent, count_got,
    vox_sent, vox_got, votes_sent, votes_got,
    count_ss, count_rs, vox_ss, vox_rs, one_ss, one_rs, two_ss, two_rs, vote_ss, vote_rs,
    *, groups, tiles,
):
    me, tile = lax.axis_index("grp"), lax.axis_index("tile")
    chans = nodes.shape[0]
    chunks = start.shape[1]
    block = chunks * WIN
    run = WIN // groups
    rows = groups * WIN
    count = count_ref[0]

    barrier = pltpu.get_barrier_semaphore()
    for d in range(1, groups):
        pl.semaphore_signal(barrier, inc=1, device_id=(lax.rem(me + d, groups), tile), device_id_type=MESH)
    for d in range(1, tiles):
        pl.semaphore_signal(barrier, inc=1, device_id=(me, lax.rem(tile + d, tiles)), device_id_type=MESH)

    def to_group(d, src, dst, ss, rs):
        return pltpu.make_async_remote_copy(
            src_ref=src, dst_ref=dst, send_sem=ss, recv_sem=rs,
            device_id=(lax.rem(me + d, groups), tile), device_id_type=MESH,
        )

    def to_tile(d, src, dst, ss, rs):
        return pltpu.make_async_remote_copy(
            src_ref=src, dst_ref=dst, send_sem=ss, recv_sem=rs,
            device_id=(me, lax.rem(tile + d, tiles)), device_id_type=MESH,
        )

    def count_copy(d):
        return to_group(d, count_sent, count_got.at[me], count_ss.at[d], count_rs.at[d])

    def vox_copy(d):
        peer = lax.rem(tile + d, tiles)
        return to_tile(d, vox_sent.at[peer], vox_got.at[tile], vox_ss.at[d], vox_rs.at[d])

    def one_copy(d, c):
        peer = lax.rem(me + d, groups)
        return to_group(d, sent_one.at[c, peer], got_one.at[c, me], one_ss.at[c, d], one_rs.at[c, d])

    def two_copy(d, c):
        peer = lax.rem(me + d, groups)
        return to_group(d, sent_two.at[c, peer], got_two.at[me, c], two_ss.at[c, d], two_rs.at[c, d])

    def vote_copy(d):
        peer = lax.rem(tile + d, tiles)
        return to_tile(d, votes_sent.at[peer], votes_got.at[tile], vote_ss.at[d], vote_rs.at[d])

    count_sent[...] = jnp.full(count_sent.shape, count, jnp.int32)
    count_got[me] = jnp.full(count_sent.shape, count, jnp.int32)
    place_positions(start, nodes, ids[...], pos_weight[...])
    in_one[...] = turned(qkv_one[...])
    in_two[...] = turned(qkv_two[...])
    proj_one[...] = turned(out_one[...])
    proj_two[...] = turned(out_two[...])
    up_turned[...] = turned(w_up[...])
    for norm, gain in ((norm_one, gain_one), (norm_two, gain_two), (norm_three, gain_three)):
        norm[...] = jnp.broadcast_to(gain[...], (LANES, chans)).T

    votes = owner_ref.shape[1]
    owner = owner_ref[...].astype(F32)
    owner_col = columns(owner)
    earlier, later = iota((votes, LANES), 0), iota((votes, LANES), 1)
    ranks = []
    for t in range(votes // LANES):
        same = jnp.logical_and(owner_col == owner[:, LANES * t : LANES * t + LANES], earlier < later + LANES * t)
        ranks.append(jnp.sum(jnp.where(same, 1.0, 0.0), 0, keepdims=True))
    rank = jnp.concatenate(ranks, 1)
    place = owner * CAP + rank
    named = jnp.where(iota((tiles, votes), 0).astype(F32) == owner, voxel_ref[...].astype(F32), 0.0).astype(BF16)
    lane = iota((votes, LANES), 1)
    ranked = (columns(rank) == (lane % CAP).astype(F32)).astype(BF16)
    table = mm(named, ranked)
    share = LANES // CAP
    table = jnp.where(iota((tiles, LANES), 1) // CAP == lax.rem(tile, share), table, 0.0)
    for t in range(tiles):
        vox_sent[t] = jnp.broadcast_to(table[t : t + 1, :], vox_sent.shape[1:])
    vox_got[tile] = vox_sent[tile]

    pl.semaphore_wait(barrier, groups + tiles - 2)
    for d in range(1, groups):
        count_copy(d).start()
    for d in range(1, tiles):
        vox_copy(d).start()

    key = iota((WIN, LANES), 0)
    window = iota((WIN, LANES), 1) // WIN

    def stage_one(c, carry):
        x = jnp.concatenate([start[g, c] for g in range(groups)], 0).astype(F32)
        biases = []
        for half in range(rows // LANES):
            slot = (window + half * (LANES // WIN)) * block + c * WIN + key
            kept = jnp.where(slot < count, 1.0, 0.0)
            biases.append((kept - 1.0) * 1000000000.0)
        first = attend(x.T, biases, norm_one[...], in_one[...], proj_one[...])
        sent_one[c] = first.T.astype(BF16).reshape(groups, WIN, chans)
        got_one[c, me] = sent_one[c, me]
        for d in range(1, groups):
            one_copy(d, c).start()
        return carry

    lax.fori_loop(0, chunks, stage_one, 0)

    for d in range(1, groups):
        count_copy(d).wait_recv()
    counts = jnp.zeros((WIN, LANES), jnp.int32)
    for g in range(groups):
        counts = jnp.where(key // run == g, count_got[g][:1, :], counts)
    def stage_two(c, carry):
        for d in range(1, groups):
            one_copy(d, c).wait_recv()
        x = swapped(got_one[c].reshape(rows, chans).astype(F32), groups).T
        biases = []
        for half in range(rows // LANES):
            slot = me * block + c * WIN + (half * (LANES // WIN) + window) * run + key % run
            kept = jnp.where(slot < counts, 1.0, 0.0)
            biases.append((kept - 1.0) * 1000000000.0)
        second = attend(x, biases, norm_two[...], in_two[...], proj_two[...])
        third = feed(second, norm_three[...], up_turned[...], w_down[...])
        sent_two[c] = swapped(third.T, groups).astype(BF16).reshape(groups, WIN, chans)
        got_two[me, c] = sent_two[c, me]
        for d in range(1, groups):
            two_copy(d, c).start()
        return carry

    lax.fori_loop(0, chunks, stage_two, 0)

    slots = nodes.shape[1]
    slot_col = columns(slot_ref[...])
    chosen = jnp.concatenate(
        [(slot_col == (lane + LANES * t).astype(F32)).astype(BF16) for t in range(slots // LANES)], 1
    )
    for d in range(1, tiles):
        vox_copy(d).wait_recv()
    vox = iota((VOX_DEV, LANES), 0).astype(F32)
    sums = []
    for a in range(tiles // share):
        mine = vox_got[share * a]
        for u in range(1, share):
            mine = mine + vox_got[share * a + u]
        sums.append((vox == mine[:1, :]).astype(BF16))
    sums = jnp.concatenate(sums, 1)

    for c in range(chunks):
        for d in range(1, groups):
            two_copy(d, c).wait_recv()
    back = got_two[...].reshape(slots, chans)
    feat = jnp.where(iota((slots, chans), 0) < count, back.astype(F32), 0.0).astype(BF16)
    feat_out[...] = feat.astype(F32).T.astype(BF16)
    picked = mm(chosen, feat).astype(BF16)
    packing = (iota((tiles * CAP, votes), 0).astype(F32) == place).astype(BF16)
    votes_sent[...] = mm(packing, picked).astype(BF16).reshape(tiles, CAP, chans)
    votes_got[tile] = votes_sent[tile]
    for d in range(1, tiles):
        vote_copy(d).start()
    for d in range(1, tiles):
        vote_copy(d).wait_recv()
    vox_out[...] = mm(sums, votes_got[...].reshape(tiles * CAP, chans)).T

    for d in range(1, groups):
        count_copy(d).wait_send()
        for c in range(chunks):
            one_copy(d, c).wait_send()
            two_copy(d, c).wait_send()
    for d in range(1, tiles):
        vox_copy(d).wait_send()
        vote_copy(d).wait_send()


def body(
    nodes, node_ids, node_count, pos_weight, gain_one, qkv_one, out_one, gain_two, qkv_two, out_two,
    gain_three, w_up, w_down, vote_slot, vote_owner, vote_voxel,
):
    slots, chans = nodes.shape
    votes = vote_slot.shape[0]
    groups, tiles = lax.axis_size("grp"), lax.axis_size("tile")
    chunks = slots // groups // WIN
    vmem = pl.BlockSpec(memory_space=pltpu.VMEM)
    dma = pltpu.SemaphoreType.DMA


    feat, sums = pl.pallas_call(
        functools.partial(kernel, groups=groups, tiles=tiles),
        out_shape=(
            jax.ShapeDtypeStruct((chans, slots), BF16),
            jax.ShapeDtypeStruct((chans, VOX_DEV), F32),
        ),
        in_specs=[pl.BlockSpec(memory_space=pltpu.SMEM)] + [vmem] * 15,
        out_specs=(vmem, vmem),
        scratch_shapes=[
            pltpu.VMEM((groups, chunks, WIN, chans), BF16),
            pltpu.VMEM((3 * chans, chans), BF16),
            pltpu.VMEM((chans, chans), BF16),
            pltpu.VMEM((3 * chans, chans), BF16),
            pltpu.VMEM((chans, chans), BF16),
            pltpu.VMEM((w_up.shape[1], chans), BF16),
            pltpu.VMEM((chans, LANES), F32),
            pltpu.VMEM((chans, LANES), F32),
            pltpu.VMEM((chans, LANES), F32),
            pltpu.VMEM((chunks, groups, WIN, chans), BF16),
            pltpu.VMEM((chunks, groups, WIN, chans), BF16),
            pltpu.VMEM((chunks, groups, WIN, chans), BF16),
            pltpu.VMEM((groups, chunks, WIN, chans), BF16),
            pltpu.VMEM((8, LANES), jnp.int32),
            pltpu.VMEM((groups, 8, LANES), jnp.int32),
            pltpu.VMEM((tiles, 8, LANES), F32),
            pltpu.VMEM((tiles, 8, LANES), F32),
            pltpu.VMEM((tiles, CAP, chans), BF16),
            pltpu.VMEM((tiles, CAP, chans), BF16),
            dma((groups,)), dma((groups,)), dma((tiles,)), dma((tiles,)),
            dma((chunks, groups)), dma((chunks, groups)), dma((chunks, groups)), dma((chunks, groups)),
            dma((tiles,)), dma((tiles,)),
        ],
        compiler_params=pltpu.CompilerParams(collective_id=0, has_side_effects=True),
    )(
        node_count, nodes.T, node_ids.reshape(slots // LANES, LANES), pos_weight,
        gain_one.reshape(1, chans), qkv_one, out_one, gain_two.reshape(1, chans), qkv_two, out_two,
        gain_three.reshape(1, chans), w_up, w_down.T,
        vote_slot.reshape(1, votes), vote_owner.reshape(1, votes), vote_voxel.reshape(1, votes),
    )
    return feat.T.astype(F32), sums.T


def solution(mesh):
    in_specs = (
        P(("grp", "tile"), None),
        P(("grp", "tile")),
        P(("grp", "tile")),
        P(),
        P(),
        P(),
        P(),
        P(),
        P(),
        P(),
        P(),
        P(),
        P(),
        P(("grp", "tile")),
        P(("grp", "tile"), None),
        P(("grp", "tile")),
    )
    out_specs = (P(("grp", "tile"), None), P(("grp", "tile"), None))
    return jax.shard_map(body, mesh=mesh, in_specs=in_specs, out_specs=out_specs, check_vma=False)
```

```python
import functools
import jax
import jax.numpy as jnp
from jax import lax
from jax.experimental import pallas as pl
from jax.experimental.pallas import tpu as pltpu
from jax.sharding import PartitionSpec as P

HEADS = 12
WIN = 32
VOX_DEV = 256
CAP = 32
LANES = 128
F32 = jnp.float32
BF16 = jnp.bfloat16
NT = (((1,), (1,)), ((), ()))
TN = (((0,), (0,)), ((), ()))
MESH = pl.DeviceIdType.MESH
LOG2E = 1.4426950408889634
ENTER = 2
VMEM_LIMIT = 24 * 2**20


def spread_order(tiles):
    return range(1, tiles)


def iota(shape, dim):
    return lax.broadcasted_iota(jnp.int32, shape, dim)


def mm(a, b, dims=(((1,), (0,)), ((), ()))):
    return lax.dot_general(a, b, dims, preferred_element_type=F32)


def normed(x, gain):
    mean = jnp.mean(x, 0, keepdims=True)
    var = jnp.mean((x - mean) ** 2, 0, keepdims=True)
    return ((x - mean) * lax.rsqrt(var + 1e-05) * jnp.concatenate([gain] * (x.shape[1] // LANES), 1)).astype(BF16)


def attend(x, biases, gain, w_qkv, w_out):
    chans = x.shape[0]
    dim = chans // HEADS
    wins = LANES // WIN
    qkv = mm(w_qkv, normed(x, gain))
    query = (qkv[:chans] * (dim**-0.5 * LOG2E)).astype(BF16)
    keys = qkv[chans : 2 * chans].astype(BF16)
    values = qkv[2 * chans :].astype(BF16)
    lane_win = iota((WIN, LANES), 1) // WIN
    own = [lane_win == w for w in range(wins)]
    own_short = [m[:dim] for m in own]
    zero = jnp.zeros((dim, LANES), BF16)
    pairs = [(half, first) for half in range(len(biases)) for first in range(0, HEADS, 2)]
    scores = {}
    for half, first in pairs:
        lanes = slice(LANES * half, LANES * half + LANES)
        rows = slice(first * dim, first * dim + 2 * dim)
        two = query[rows, lanes]
        blocks = jnp.concatenate(
            [jnp.concatenate([two[:dim], zero], 1), jnp.concatenate([zero, two[dim:]], 1)], 0
        )
        full = mm(keys[rows, lanes], blocks, TN)
        for i in range(2):
            wide = full[:, LANES * i : LANES * i + LANES]
            picked = wide[:WIN]
            for w in range(1, wins):
                picked = jnp.where(own[w], wide[WIN * w : WIN * w + WIN], picked)
            scores[half, first + i] = picked + biases[half]
    probs, totals = {}, {}
    for key, score in scores.items():
        weights = jnp.exp2(score - jnp.max(score, 0, keepdims=True))
        totals[key] = 1.0 / jnp.sum(weights, 0, keepdims=True)
        probs[key] = weights.astype(BF16)
    context = {}
    for half, first in pairs:
        rows = slice(first * dim, first * dim + 2 * dim)
        stacked = jnp.concatenate(
            [values[rows, LANES * half + WIN * w : LANES * half + WIN * w + WIN] for w in range(wins)], 0
        )
        mixed = mm(stacked, jnp.concatenate([probs[half, first], probs[half, first + 1]], 1))
        for i in range(2):
            wide = mixed[:, LANES * i : LANES * i + LANES]
            at = [2 * dim * w + dim * i for w in range(wins)]
            picked = wide[at[0] : at[0] + dim]
            for w in range(1, wins):
                picked = jnp.where(own_short[w], wide[at[w] : at[w] + dim], picked)
            context[half, first + i] = (picked * totals[half, first + i]).astype(BF16)
    merged = jnp.concatenate(
        [jnp.concatenate([context[half, h] for h in range(HEADS)], 0) for half in range(len(biases))], 1
    )
    return x + mm(w_out, merged)


def feed(x, gain, w_up, w_down):
    up = mm(w_up, normed(x, gain))
    inside = up * (0.7978845608028654 + 0.035677408136300125 * up * up)
    hidden = (0.5 * up * (1.0 + jnp.tanh(inside))).astype(BF16)
    return x + mm(w_down, hidden)


def swapped(x, groups):
    half = x.shape[0] // groups // 2
    run = WIN // groups
    parts = x.reshape(groups // 2, 2, groups // 2, 2 * run, x.shape[1])
    low = iota((2 * run, x.shape[1]), 0) < run
    out = []
    for b in range(groups // 2):
        for odd in range(2):
            for a in range(groups // 2):
                first, second = parts[a, 0, b], parts[a, 1, b]
                if odd:
                    out.append(jnp.where(low, pltpu.roll(first, run, 0), second))
                else:
                    out.append(jnp.where(low, first, pltpu.roll(second, run, 0)))
    return jnp.concatenate(out, 0)


def turned(w):
    return w.astype(F32).T.astype(BF16)


def columns(row):
    parts = []
    for t in range(row.shape[1] // LANES):
        piece = row[:, LANES * t : LANES * t + LANES].astype(F32)
        parts.append(jnp.broadcast_to(piece, (LANES, LANES)).T)
    return jnp.concatenate(parts, 0)


def place_positions(start, nodes, ids, pos_weight):
    groups, chunks, win, chans = start.shape
    row = iota((16, chans), 0)
    pick = [pos_weight[a : a + 1, :] for a in range(3)]
    spread = jnp.where(row % 3 == 0, pick[0], jnp.where(row % 3 == 1, pick[1], pick[2]))
    high = spread.astype(BF16).astype(F32)
    middle = (spread - high).astype(BF16).astype(F32)
    low = spread - high - middle
    split = jnp.where(row < 3, high, jnp.where(row < 6, middle, jnp.where(row < 9, low, 0.0))).astype(BF16)
    axes = []
    for axis in range(3):
        total = jnp.zeros(ids.shape, jnp.int32)
        for level in range(6):
            total = total + jnp.bitwise_and(jnp.right_shift(ids, 3 * level + axis), 1) * 2**level
        axes.append(total.astype(F32) / 64.0 - 0.5)
    slim = iota((16, LANES), 0)
    for g in range(groups):
        line = [a[g : g + 1, :] for a in axes]
        coords = jnp.where(slim % 3 == 0, line[0], jnp.where(slim % 3 == 1, line[1], line[2])).astype(BF16)
        moved = nodes[:, LANES * g : LANES * g + LANES].astype(F32) + mm(split, coords, TN)
        start[g] = moved.T.astype(BF16).reshape(chunks, win, chans)


def kernel(
    count_ref, nodes, ids, pos_weight, gain_one, qkv_one, out_one, gain_two, qkv_two, out_two,
    gain_three, w_up, w_down, slot_ref, owner_ref, voxel_ref,
    feat_out, vox_out,
    start, in_one, proj_one, in_two, proj_two, up_turned, norm_one, norm_two, norm_three,
    sent_one, got_one, sent_two, got_two, count_sent, count_got, vox_sent, vox_got, votes_sent, votes_got,
    count_ss, count_rs, vox_ss, vox_rs, one_ss, one_rs, two_ss, two_rs, vote_ss, vote_rs, known,
    *, groups, tiles,
):
    me, tile = lax.axis_index("grp"), lax.axis_index("tile")
    chans, slots = nodes.shape
    chunks = start.shape[1]
    block = chunks * WIN
    run = WIN // groups
    rows = groups * WIN
    count = count_ref[0]
    steps = [2**i for i in range(tiles.bit_length() - 1)]

    def across(step):
        return tile + step - 2 * step * lax.rem(tile // step, 2)

    def grp_peer(d):
        return lax.rem(me + d, groups)

    def tile_peer(d):
        return lax.rem(tile + d, tiles)

    barrier = pltpu.get_barrier_semaphore()
    for d in range(1, groups):
        pl.semaphore_signal(barrier, inc=1, device_id=(grp_peer(d), tile), device_id_type=MESH)
    for step in steps:
        pl.semaphore_signal(barrier, inc=1, device_id=(me, across(step)), device_id_type=MESH)

    def tell(i):
        pl.semaphore_signal(known.at[i], inc=1, device_id=(me, across(steps[i])), device_id_type=MESH)

    def told(i):
        pl.semaphore_wait(known.at[i], 1)

    def to_group(d, src, dst, ss, rs):
        pltpu.make_async_remote_copy(
            src_ref=src, dst_ref=dst, send_sem=ss, recv_sem=rs,
            device_id=(grp_peer(d), tile), device_id_type=MESH,
        ).start()

    def to_tile(d, src, dst, ss, rs):
        pltpu.make_async_remote_copy(
            src_ref=src, dst_ref=dst, send_sem=ss, recv_sem=rs,
            device_id=(me, tile_peer(d)), device_id_type=MESH,
        ).start()

    def settle(ref, sem):
        pltpu.make_async_copy(ref, ref, sem).wait()

    def send_one(c):
        for d in range(1, groups):
            to_group(d, sent_one.at[c, grp_peer(d)], got_one.at[c, me], one_ss, one_rs.at[c])

    others = pl.ds(0, groups - 1)
    rest = pl.ds(0, tiles - 1)

    count_sent[...] = jnp.full(count_sent.shape, count, jnp.int32)
    count_got[me] = jnp.full(count_sent.shape, count, jnp.int32)
    place_positions(start, nodes, ids[...], pos_weight[...])
    in_one[...] = turned(qkv_one[...])
    proj_one[...] = turned(out_one[...])
    norm_one[...] = jnp.broadcast_to(gain_one[...], (LANES, chans)).T

    key = iota((WIN, LANES), 0)
    window = iota((WIN, LANES), 1) // WIN

    def stage_one(c, carry):
        x = jnp.concatenate([start[g, c] for g in range(groups)], 0).astype(F32)
        biases = []
        for half in range(rows // LANES):
            slot = (window + half * (LANES // WIN)) * block + c * WIN + key
            kept = jnp.where(slot < count, 1.0, 0.0)
            biases.append((kept - 1.0) * 1000000000.0)
        first = attend(x.T, biases, norm_one[...], in_one[...], proj_one[...])
        sent_one[c] = first.T.astype(BF16).reshape(groups, WIN, chans)
        got_one[c, me] = sent_one[c, me]

        @pl.when(c == ENTER)
        def _():
            pl.semaphore_wait(barrier, groups - 1 + len(steps))
            for earlier in range(ENTER):
                send_one(earlier)
            for d in range(1, groups):
                to_group(d, count_sent, count_got.at[me], count_ss, count_rs)
            tell(1)

        @pl.when(c >= ENTER)
        def _():
            send_one(c)

        return carry

    lax.fori_loop(0, chunks, stage_one, 0)
    told(1)
    tell(2)

    in_two[...] = turned(qkv_two[...])
    proj_two[...] = turned(out_two[...])
    up_turned[...] = turned(w_up[...])
    for norm, gain in ((norm_two, gain_two), (norm_three, gain_three)):
        norm[...] = jnp.broadcast_to(gain[...], (LANES, chans)).T
    votes = owner_ref.shape[1]
    owner = owner_ref[...].astype(F32)
    owner_col = columns(owner)
    earlier, later = iota((votes, LANES), 0), iota((votes, LANES), 1)
    ranks = []
    for t in range(votes // LANES):
        same = jnp.logical_and(owner_col == owner[:, LANES * t : LANES * t + LANES], earlier < later + LANES * t)
        ranks.append(jnp.sum(jnp.where(same, 1.0, 0.0), 0, keepdims=True))
    rank = jnp.concatenate(ranks, 1)
    place = owner * CAP + rank
    named = jnp.where(iota((tiles, votes), 0).astype(F32) == owner, voxel_ref[...].astype(F32), 0.0).astype(BF16)
    lane = iota((votes, LANES), 1)
    ranked = (columns(rank) == (lane % CAP).astype(F32)).astype(BF16)
    table = mm(named, ranked)
    share = LANES // CAP
    table = jnp.where(iota((tiles, LANES), 1) // CAP == lax.rem(tile, share), table, 0.0)
    for t in range(tiles):
        vox_sent[t] = jnp.broadcast_to(table[t : t + 1, :], vox_sent.shape[1:])
    vox_got[tile] = vox_sent[tile]
    told(2)
    tell(3)

    settle(count_got.at[others], count_rs)
    counts = jnp.zeros((WIN, LANES), jnp.int32)
    for g in range(groups):
        counts = jnp.where(key // run == g, count_got[g][:1, :], counts)

    def stage_two(c, carry):
        settle(got_one.at[c, others], one_rs.at[c])
        x = swapped(got_one[c].reshape(rows, chans).astype(F32), groups).T
        biases = []
        for half in range(rows // LANES):
            slot = me * block + c * WIN + (half * (LANES // WIN) + window) * run + key % run
            kept = jnp.where(slot < counts, 1.0, 0.0)
            biases.append((kept - 1.0) * 1000000000.0)
        second = attend(x, biases, norm_two[...], in_two[...], proj_two[...])
        third = feed(second, norm_three[...], up_turned[...], w_down[...])
        sent_two[c] = swapped(third.T, groups).astype(BF16).reshape(groups, WIN, chans)
        got_two[me, c] = sent_two[c, me]
        for d in range(1, groups):
            to_group(d, sent_two.at[c, grp_peer(d)], got_two.at[me, c], two_ss, two_rs.at[c])

        @pl.when(c == 0)
        def _():
            told(3)
            tell(4)

        @pl.when(c == 1)
        def _():
            told(4)
            for d in range(1, tiles):
                to_tile(d, vox_sent.at[tile_peer(d)], vox_got.at[tile], vox_ss, vox_rs)

        return carry

    lax.fori_loop(0, chunks, stage_two, 0)

    slot_col = columns(slot_ref[...])

    def pick(c):
        chosen = []
        for t in range(rows // LANES):
            slot = (t * (LANES // WIN) + lane // WIN) * block + c * WIN + lane % WIN
            chosen.append((slot_col == slot.astype(F32)).astype(BF16))
        line = iota((rows, chans), 0)
        kept = line // WIN * block + c * WIN + line % WIN < count
        part = jnp.where(kept, got_two[:, c].reshape(rows, chans).astype(F32), 0.0).astype(BF16)
        return mm(jnp.concatenate(chosen, 1), part)

    settle(vox_got.at[rest], vox_rs)
    vox = iota((VOX_DEV, LANES), 0).astype(F32)
    sums = []
    for a in range(tiles // share):
        mine = vox_got[share * a]
        for u in range(1, share):
            mine = mine + vox_got[share * a + u]
        sums.append((vox == mine[:1, :]).astype(BF16))
    sums = jnp.concatenate(sums, 1)
    packing = (iota((tiles * CAP, votes), 0).astype(F32) == place).astype(BF16)
    picked = None
    for c in range(chunks):
        settle(got_two.at[others, c], two_rs.at[c])
        part = pick(c)
        picked = part if picked is None else picked + part
    picked = picked.astype(BF16)

    per = tiles // 4
    short = chans - LANES
    for q in range(4):
        mine = mm(packing[q * per * CAP : (q + 1) * per * CAP], picked).reshape(per, CAP, chans)
        tail = mine[:, :, LANES:]
        tail = jnp.concatenate([tail[:, : CAP // 2], tail[:, CAP // 2 :]], 2)
        votes_sent[q * per : (q + 1) * per] = jnp.concatenate([mine[:, :, :LANES], tail], 1).astype(BF16)
    votes_got[tile] = votes_sent[tile]
    for d in spread_order(tiles):
        to_tile(d, votes_sent.at[tile_peer(d)], votes_got.at[tile], vote_ss, vote_rs)

    back = got_two[...].reshape(slots, chans)
    feat = jnp.where(iota((slots, chans), 0) < count, back.astype(F32), 0.0)
    feat_out[...] = feat.T.astype(BF16)
    settle(count_got.at[others], count_ss)
    settle(got_one.at[:, others], one_ss)
    settle(got_two.at[others, :], two_ss)
    settle(vox_got.at[rest], vox_ss)
    settle(votes_got.at[rest], vote_ss)

    settle(votes_got.at[rest], vote_rs)
    head = votes_got[:, :CAP, :].reshape(tiles * CAP, LANES)
    tail = votes_got[:, CAP:, :].astype(F32)
    tail = jnp.concatenate([tail[:, :, :short], tail[:, :, short:]], 1).reshape(tiles * CAP, short).astype(BF16)
    vox_out[...] = mm(sums, jnp.concatenate([head, tail], 1)).T


def finish(feat, sums, feat_out, sums_out):
    feat_out[...] = feat[...].astype(F32)
    sums_out[...] = sums[...]


def body(
    nodes, node_ids, node_count, pos_weight, gain_one, qkv_one, out_one, gain_two, qkv_two, out_two,
    gain_three, w_up, w_down, vote_slot, vote_owner, vote_voxel,
):
    slots, chans = nodes.shape
    votes = vote_slot.shape[0]
    groups, tiles = lax.axis_size("grp"), lax.axis_size("tile")
    chunks = slots // groups // WIN
    vmem = pl.BlockSpec(memory_space=pltpu.VMEM)
    dma = pltpu.SemaphoreType.DMA


    feat, sums = pl.pallas_call(
        functools.partial(kernel, groups=groups, tiles=tiles),
        out_shape=(
            jax.ShapeDtypeStruct((chans, slots), BF16),
            jax.ShapeDtypeStruct((chans, VOX_DEV), F32),
        ),
        in_specs=[pl.BlockSpec(memory_space=pltpu.SMEM)] + [vmem] * 15,
        out_specs=(vmem, vmem),
        scratch_shapes=[
            pltpu.VMEM((groups, chunks, WIN, chans), BF16),
            pltpu.VMEM((3 * chans, chans), BF16),
            pltpu.VMEM((chans, chans), BF16),
            pltpu.VMEM((3 * chans, chans), BF16),
            pltpu.VMEM((chans, chans), BF16),
            pltpu.VMEM((w_up.shape[1], chans), BF16),
            pltpu.VMEM((chans, LANES), F32),
            pltpu.VMEM((chans, LANES), F32),
            pltpu.VMEM((chans, LANES), F32),
            pltpu.VMEM((chunks, groups, WIN, chans), BF16),
            pltpu.VMEM((chunks, groups, WIN, chans), BF16),
            pltpu.VMEM((chunks, groups, WIN, chans), BF16),
            pltpu.VMEM((groups, chunks, WIN, chans), BF16),
            pltpu.VMEM((8, LANES), jnp.int32),
            pltpu.VMEM((groups, 8, LANES), jnp.int32),
            pltpu.VMEM((tiles, 8, LANES), F32),
            pltpu.VMEM((tiles, 8, LANES), F32),
            pltpu.VMEM((tiles, CAP * 3 // 2, LANES), BF16),
            pltpu.VMEM((tiles, CAP * 3 // 2, LANES), BF16),
            dma, dma, dma, dma, dma, dma((chunks,)), dma, dma((chunks,)), dma, dma,
            pltpu.SemaphoreType.REGULAR((tiles.bit_length() - 1,)),
        ],
        compiler_params=pltpu.CompilerParams(collective_id=0, has_side_effects=True, vmem_limit_bytes=VMEM_LIMIT),
    )(
        node_count, nodes.T, node_ids.reshape(slots // LANES, LANES), pos_weight,
        gain_one.reshape(1, chans), qkv_one, out_one, gain_two.reshape(1, chans), qkv_two, out_two,
        gain_three.reshape(1, chans), w_up, w_down.T,
        vote_slot.reshape(1, votes), vote_owner.reshape(1, votes), vote_voxel.reshape(1, votes),
    )
    feat, sums = pl.pallas_call(
        finish,
        out_shape=(
            jax.ShapeDtypeStruct((chans, slots), F32),
            jax.ShapeDtypeStruct((chans, VOX_DEV), F32),
        ),
        in_specs=[vmem, vmem],
        out_specs=(vmem, vmem),
        compiler_params=pltpu.CompilerParams(vmem_limit_bytes=8 * 2**20),
    )(feat, sums)
    return feat.T, sums.T


def solution(mesh):
    in_specs = (
        P(("grp", "tile"), None),
        P(("grp", "tile")),
        P(("grp", "tile")),
        P(),
        P(),
        P(),
        P(),
        P(),
        P(),
        P(),
        P(),
        P(),
        P(),
        P(("grp", "tile")),
        P(("grp", "tile"), None),
        P(("grp", "tile")),
    )
    out_specs = (P(("grp", "tile"), None), P(("grp", "tile"), None))
    return jax.shard_map(body, mesh=mesh, in_specs=in_specs, out_specs=out_specs, check_vma=False)
```

```python
import functools
import jax
import jax.numpy as jnp
from jax import lax
from jax.experimental import pallas as pl
from jax.experimental.pallas import tpu as pltpu
from jax.sharding import PartitionSpec as P

HEADS = 12
WIN = 32
VOX_DEV = 256
CAP = 32
LANES = 128
F32 = jnp.float32
BF16 = jnp.bfloat16
NT = (((1,), (1,)), ((), ()))
TN = (((0,), (0,)), ((), ()))
MESH = pl.DeviceIdType.MESH
LOG2E = 1.4426950408889634
ENTER = 2
INPUTS = 15
FIRST = (0, 1, 2, 4, 5, 3)
LATER = (7, 8, 6, 9, 10, 11, 13, 14, 12)


ROWS = 4


def by_distance(n):
    return sorted(range(n), key=lambda d: (-min(d, n - d), d))


def iota(shape, dim):
    return lax.broadcasted_iota(jnp.int32, shape, dim)


def mm(a, b, dims=(((1,), (0,)), ((), ()))):
    return lax.dot_general(a, b, dims, preferred_element_type=F32)


def normed(x, gain):
    mean = jnp.mean(x, 0, keepdims=True)
    var = jnp.mean((x - mean) ** 2, 0, keepdims=True)
    return ((x - mean) * lax.rsqrt(var + 1e-05) * jnp.concatenate([gain] * (x.shape[1] // LANES), 1)).astype(BF16)


def attend(x, biases, gain, w_qkv, w_out):
    chans = x.shape[0]
    dim = chans // HEADS
    wins = LANES // WIN
    qkv = mm(w_qkv, normed(x, gain))
    query = (qkv[:chans] * (dim**-0.5 * LOG2E)).astype(BF16)
    keys = qkv[chans : 2 * chans].astype(BF16)
    values = qkv[2 * chans :].astype(BF16)
    lane_win = iota((WIN, LANES), 1) // WIN
    own = [lane_win == w for w in range(wins)]
    own_short = [m[:dim] for m in own]
    zero = jnp.zeros((dim, LANES), BF16)
    pairs = [(half, first) for half in range(len(biases)) for first in range(0, HEADS, 2)]
    scores = {}
    for half, first in pairs:
        lanes = slice(LANES * half, LANES * half + LANES)
        rows = slice(first * dim, first * dim + 2 * dim)
        two = query[rows, lanes]
        blocks = jnp.concatenate(
            [jnp.concatenate([two[:dim], zero], 1), jnp.concatenate([zero, two[dim:]], 1)], 0
        )
        full = mm(keys[rows, lanes], blocks, TN)
        for i in range(2):
            wide = full[:, LANES * i : LANES * i + LANES]
            picked = wide[:WIN]
            for w in range(1, wins):
                picked = jnp.where(own[w], wide[WIN * w : WIN * w + WIN], picked)
            scores[half, first + i] = picked + biases[half]
    probs, totals = {}, {}
    for key, score in scores.items():
        weights = jnp.exp2(score - jnp.max(score, 0, keepdims=True))
        totals[key] = 1.0 / jnp.sum(weights, 0, keepdims=True)
        probs[key] = weights.astype(BF16)
    context = {}
    for half, first in pairs:
        rows = slice(first * dim, first * dim + 2 * dim)
        stacked = jnp.concatenate(
            [values[rows, LANES * half + WIN * w : LANES * half + WIN * w + WIN] for w in range(wins)], 0
        )
        mixed = mm(stacked, jnp.concatenate([probs[half, first], probs[half, first + 1]], 1))
        for i in range(2):
            wide = mixed[:, LANES * i : LANES * i + LANES]
            at = [2 * dim * w + dim * i for w in range(wins)]
            picked = wide[at[0] : at[0] + dim]
            for w in range(1, wins):
                picked = jnp.where(own_short[w], wide[at[w] : at[w] + dim], picked)
            context[half, first + i] = (picked * totals[half, first + i]).astype(BF16)
    merged = jnp.concatenate(
        [jnp.concatenate([context[half, h] for h in range(HEADS)], 0) for half in range(len(biases))], 1
    )
    return x + mm(w_out, merged)


def feed(x, gain, w_up, w_down):
    up = mm(w_up, normed(x, gain))
    inside = up * (0.7978845608028654 + 0.035677408136300125 * up * up)
    hidden = (0.5 * up * (1.0 + jnp.tanh(inside))).astype(BF16)
    return x + mm(w_down, hidden)


def swapped(x, groups):
    half = x.shape[0] // groups // 2
    run = WIN // groups
    parts = x.reshape(groups // 2, 2, groups // 2, 2 * run, x.shape[1])
    low = iota((2 * run, x.shape[1]), 0) < run
    out = []
    for b in range(groups // 2):
        for odd in range(2):
            for a in range(groups // 2):
                first, second = parts[a, 0, b], parts[a, 1, b]
                if odd:
                    out.append(jnp.where(low, pltpu.roll(first, run, 0), second))
                else:
                    out.append(jnp.where(low, first, pltpu.roll(second, run, 0)))
    return jnp.concatenate(out, 0)


def turned(w):
    return w.astype(F32).T.astype(BF16)


def columns(row):
    parts = []
    for t in range(row.shape[1] // LANES):
        piece = row[:, LANES * t : LANES * t + LANES].astype(F32)
        parts.append(jnp.broadcast_to(piece, (LANES, LANES)).T)
    return jnp.concatenate(parts, 0)


def place_positions(start, nodes, ids, pos_weight):
    groups, chunks, win, chans = start.shape
    row = iota((16, chans), 0)
    pick = [pos_weight[a : a + 1, :] for a in range(3)]
    spread = jnp.where(row % 3 == 0, pick[0], jnp.where(row % 3 == 1, pick[1], pick[2]))
    high = spread.astype(BF16).astype(F32)
    middle = (spread - high).astype(BF16).astype(F32)
    low = spread - high - middle
    split = jnp.where(row < 3, high, jnp.where(row < 6, middle, jnp.where(row < 9, low, 0.0))).astype(BF16)
    axes = []
    for axis in range(3):
        total = jnp.zeros(ids.shape, jnp.int32)
        for level in range(6):
            total = total + jnp.bitwise_and(jnp.right_shift(ids, 3 * level + axis), 1) * 2**level
        axes.append(total.astype(F32) / 64.0 - 0.5)
    slim = iota((16, LANES), 0)
    for g in range(groups):
        line = [a[g : g + 1, :] for a in axes]
        coords = jnp.where(slim % 3 == 0, line[0], jnp.where(slim % 3 == 1, line[1], line[2])).astype(BF16)
        moved = nodes[:, LANES * g : LANES * g + LANES].astype(F32) + mm(split, coords, TN)
        start[g] = moved.T.astype(BF16).reshape(chunks, win, chans)


def kernel(
    count_ref, *refs, groups, tiles,
):
    far, (feat_out, vox_out), near = refs[:INPUTS], refs[INPUTS : INPUTS + 2], refs[INPUTS + 2 : 2 * INPUTS + 2]
    (
        nodes, ids, pos_weight, gain_one, qkv_one, out_one, gain_two, qkv_two, out_two,
        gain_three, w_up, w_down, slot_ref, owner_ref, voxel_ref,
    ) = near
    loads = refs[2 * INPUTS + 2]
    (
    start, in_one, proj_one, in_two, proj_two, up_turned, norm_one, norm_two, norm_three,
    sent_one, got_one, sent_two, got_two, count_sent, count_got, vox_sent, vox_got, votes_sent, votes_got,
    count_ss, count_rs, vox_ss, vox_rs, one_ss, one_rs, two_ss, two_rs, vote_ss, vote_rs, known, turned_feat, feat_sem,
    ) = refs[2 * INPUTS + 3 :]
    me, tile = lax.axis_index("grp"), lax.axis_index("tile")
    chans, slots = nodes.shape
    chunks = start.shape[1]
    block = chunks * WIN
    run = WIN // groups
    rows = groups * WIN
    count = count_ref[0]
    steps = [2**i for i in range(tiles.bit_length() - 1)]

    def across(step):
        return tile + step - 2 * step * lax.rem(tile // step, 2)

    def grp_peer(d):
        return lax.rem(me + d, groups)

    def tile_peer(d):
        return lax.rem(tile + d, tiles)

    barrier = pltpu.get_barrier_semaphore()
    for d in range(1, groups):
        pl.semaphore_signal(barrier, inc=1, device_id=(grp_peer(d), tile), device_id_type=MESH)
    for step in steps:
        pl.semaphore_signal(barrier, inc=1, device_id=(me, across(step)), device_id_type=MESH)

    for i in FIRST + LATER:
        pltpu.make_async_copy(far[i], near[i], loads.at[i]).start()

    def loaded(which):
        for i in which:
            pltpu.make_async_copy(far[i], near[i], loads.at[i]).wait()

    def tell(i):
        pl.semaphore_signal(known.at[i], inc=1, device_id=(me, across(steps[i])), device_id_type=MESH)

    def told(i):
        pl.semaphore_wait(known.at[i], 1)

    def to_group(d, src, dst, ss, rs):
        pltpu.make_async_remote_copy(
            src_ref=src, dst_ref=dst, send_sem=ss, recv_sem=rs,
            device_id=(grp_peer(d), tile), device_id_type=MESH,
        ).start()

    def to_tile(peer, src, dst, ss, rs):
        pltpu.make_async_remote_copy(
            src_ref=src, dst_ref=dst, send_sem=ss, recv_sem=rs,
            device_id=(me, peer), device_id_type=MESH,
        ).start()

    def settle(ref, sem):
        pltpu.make_async_copy(ref, ref, sem).wait()

    def send_one(c):
        for d in range(1, groups):
            to_group(d, sent_one.at[c, grp_peer(d)], got_one.at[c, me], one_ss, one_rs.at[c])

    others = pl.ds(0, groups - 1)
    rest = pl.ds(0, tiles - 1)

    loaded(FIRST)
    count_sent[...] = jnp.full(count_sent.shape, count, jnp.int32)
    count_got[me] = jnp.full(count_sent.shape, count, jnp.int32)
    place_positions(start, nodes, ids[...], pos_weight[...])
    in_one[...] = turned(qkv_one[...])
    proj_one[...] = turned(out_one[...])
    norm_one[...] = jnp.broadcast_to(gain_one[...], (LANES, chans)).T

    key = iota((WIN, LANES), 0)
    window = iota((WIN, LANES), 1) // WIN

    def stage_one(c, carry):
        x = jnp.concatenate([start[g, c] for g in range(groups)], 0).astype(F32)
        biases = []
        for half in range(rows // LANES):
            slot = (window + half * (LANES // WIN)) * block + c * WIN + key
            kept = jnp.where(slot < count, 1.0, 0.0)
            biases.append((kept - 1.0) * 1000000000.0)
        first = attend(x.T, biases, norm_one[...], in_one[...], proj_one[...])
        sent_one[c] = first.T.astype(BF16).reshape(groups, WIN, chans)
        got_one[c, me] = sent_one[c, me]

        @pl.when(c == ENTER)
        def _():
            pl.semaphore_wait(barrier, groups - 1 + len(steps))
            for earlier in range(ENTER):
                send_one(earlier)
            for d in range(1, groups):
                to_group(d, count_sent, count_got.at[me], count_ss, count_rs)
            tell(1)

        @pl.when(c >= ENTER)
        def _():
            send_one(c)

        return carry

    lax.fori_loop(0, chunks, stage_one, 0)
    told(1)
    tell(2)

    loaded(LATER)
    in_two[...] = turned(qkv_two[...])
    proj_two[...] = turned(out_two[...])
    up_turned[...] = turned(w_up[...])
    for norm, gain in ((norm_two, gain_two), (norm_three, gain_three)):
        norm[...] = jnp.broadcast_to(gain[...], (LANES, chans)).T
    votes = owner_ref.shape[1]
    owner = owner_ref[...].astype(F32)
    owner_col = columns(owner)
    earlier, later = iota((votes, LANES), 0), iota((votes, LANES), 1)
    ranks = []
    for t in range(votes // LANES):
        same = jnp.logical_and(owner_col == owner[:, LANES * t : LANES * t + LANES], earlier < later + LANES * t)
        ranks.append(jnp.sum(jnp.where(same, 1.0, 0.0), 0, keepdims=True))
    rank = jnp.concatenate(ranks, 1)
    place = owner * CAP + rank
    named = jnp.where(iota((tiles, votes), 0).astype(F32) == owner, voxel_ref[...].astype(F32), 0.0).astype(BF16)
    lane = iota((votes, LANES), 1)
    ranked = (columns(rank) == (lane % CAP).astype(F32)).astype(BF16)
    table = mm(named, ranked)
    share = LANES // CAP
    table = jnp.where(iota((tiles, LANES), 1) // CAP == lax.rem(tile, share), table, 0.0)
    for t in range(tiles):
        vox_sent[t] = jnp.broadcast_to(table[t : t + 1, :], vox_sent.shape[1:])
    vox_got[tile] = vox_sent[tile]
    told(2)
    tell(3)

    settle(count_got.at[others], count_rs)
    counts = jnp.zeros((WIN, LANES), jnp.int32)
    for g in range(groups):
        counts = jnp.where(key // run == g, count_got[g][:1, :], counts)

    def stage_two(c, carry):
        settle(got_one.at[c, others], one_rs.at[c])
        x = swapped(got_one[c].reshape(rows, chans).astype(F32), groups).T
        biases = []
        for half in range(rows // LANES):
            slot = me * block + c * WIN + (half * (LANES // WIN) + window) * run + key % run
            kept = jnp.where(slot < counts, 1.0, 0.0)
            biases.append((kept - 1.0) * 1000000000.0)
        second = attend(x, biases, norm_two[...], in_two[...], proj_two[...])
        third = feed(second, norm_three[...], up_turned[...], w_down[...])
        sent_two[c] = swapped(third.T, groups).astype(BF16).reshape(groups, WIN, chans)
        got_two[me, c] = sent_two[c, me]
        for d in range(1, groups):
            to_group(d, sent_two.at[c, grp_peer(d)], got_two.at[me, c], two_ss, two_rs.at[c])

        @pl.when(c == 0)
        def _():
            told(3)
            tell(4)

        @pl.when(c == 1)
        def _():
            told(4)
            for d in range(1, tiles):
                to_tile(tile_peer(d), vox_sent.at[tile_peer(d)], vox_got.at[tile], vox_ss, vox_rs)

        return carry

    lax.fori_loop(0, chunks, stage_two, 0)

    slot_col = columns(slot_ref[...])

    def pick(c):
        chosen = []
        for t in range(rows // LANES):
            slot = (t * (LANES // WIN) + lane // WIN) * block + c * WIN + lane % WIN
            chosen.append((slot_col == slot.astype(F32)).astype(BF16))
        line = iota((rows, chans), 0)
        kept = line // WIN * block + c * WIN + line % WIN < count
        part = jnp.where(kept, got_two[:, c].reshape(rows, chans).astype(F32), 0.0).astype(BF16)
        return mm(jnp.concatenate(chosen, 1), part)

    settle(vox_got.at[rest], vox_rs)
    vox = iota((VOX_DEV, LANES), 0).astype(F32)
    sums = []
    for a in range(tiles // share):
        mine = vox_got[share * a]
        for u in range(1, share):
            mine = mine + vox_got[share * a + u]
        sums.append((vox == mine[:1, :]).astype(BF16))
    sums = jnp.concatenate(sums, 1)
    picked = None
    for c in range(chunks):
        settle(got_two.at[others, c], two_rs.at[c])
        part = pick(c)
        picked = part if picked is None else picked + part
    picked = picked.astype(BF16)

    deep = tiles // ROWS
    here, along = tile // deep, lax.rem(tile, deep)
    line = iota((deep * CAP, votes), 0)
    for y in by_distance(ROWS):
        row = lax.rem(here + y, ROWS)
        packing = ((line + row * deep * CAP).astype(F32) == place).astype(BF16)
        mine = mm(packing, picked).reshape(deep, CAP, chans)
        tail = mine[:, :, LANES:]
        tail = jnp.concatenate([tail[:, : CAP // 2], tail[:, CAP // 2 :]], 2)
        votes_sent[pl.ds(row * deep, deep)] = jnp.concatenate([mine[:, :, :LANES], tail], 1).astype(BF16)
        for z in by_distance(deep):
            if y or z:
                peer = row * deep + lax.rem(along + z, deep)
                to_tile(peer, votes_sent.at[peer], votes_got.at[tile], vote_ss, vote_rs)
    votes_got[tile] = votes_sent[tile]

    short = chans - LANES
    back = got_two[...].reshape(slots, chans)
    feat = jnp.where(iota((slots, chans), 0) < count, back.astype(F32), 0.0)
    turned_feat[...] = feat.T.astype(BF16)
    leave = pltpu.make_async_copy(turned_feat, feat_out, feat_sem)
    leave.start()
    settle(count_got.at[others], count_ss)
    settle(got_one.at[:, others], one_ss)
    settle(got_two.at[others, :], two_ss)
    settle(vox_got.at[rest], vox_ss)
    settle(votes_got.at[rest], vote_ss)
    leave.wait()

    settle(votes_got.at[rest], vote_rs)
    head = votes_got[:, :CAP, :].reshape(tiles * CAP, LANES)
    tail = votes_got[:, CAP:, :].astype(F32)
    tail = jnp.concatenate([tail[:, :, :short], tail[:, :, short:]], 1).reshape(tiles * CAP, short).astype(BF16)
    vox_out[...] = mm(sums, jnp.concatenate([head, tail], 1)).T


def finish(feat, sums, feat_out, sums_out):
    feat_out[...] = feat[...].astype(F32)
    sums_out[...] = sums[...]


def body(
    nodes, node_ids, node_count, pos_weight, gain_one, qkv_one, out_one, gain_two, qkv_two, out_two,
    gain_three, w_up, w_down, vote_slot, vote_owner, vote_voxel,
):
    slots, chans = nodes.shape
    votes = vote_slot.shape[0]
    groups, tiles = lax.axis_size("grp"), lax.axis_size("tile")
    chunks = slots // groups // WIN
    vmem = pl.BlockSpec(memory_space=pltpu.VMEM)
    inputs = (
        nodes.T, node_ids.reshape(slots // LANES, LANES), pos_weight,
        gain_one.reshape(1, chans), qkv_one, out_one, gain_two.reshape(1, chans), qkv_two, out_two,
        gain_three.reshape(1, chans), w_up, w_down.T,
        vote_slot.reshape(1, votes), vote_owner.reshape(1, votes), vote_voxel.reshape(1, votes),
    )
    dma = pltpu.SemaphoreType.DMA


    feat, sums = pl.pallas_call(
        functools.partial(kernel, groups=groups, tiles=tiles),
        out_shape=(
            jax.ShapeDtypeStruct((chans, slots), BF16),
            jax.ShapeDtypeStruct((chans, VOX_DEV), F32),
        ),
        in_specs=[pl.BlockSpec(memory_space=pltpu.SMEM)] + [pl.BlockSpec(memory_space=pltpu.HBM)] * INPUTS,
        out_specs=(pl.BlockSpec(memory_space=pltpu.HBM), vmem),
        scratch_shapes=[pltpu.VMEM(i.shape, i.dtype) for i in inputs]
        + [
            dma((INPUTS,)),
            pltpu.VMEM((groups, chunks, WIN, chans), BF16),
            pltpu.VMEM((3 * chans, chans), BF16),
            pltpu.VMEM((chans, chans), BF16),
            pltpu.VMEM((3 * chans, chans), BF16),
            pltpu.VMEM((chans, chans), BF16),
            pltpu.VMEM((w_up.shape[1], chans), BF16),
            pltpu.VMEM((chans, LANES), F32),
            pltpu.VMEM((chans, LANES), F32),
            pltpu.VMEM((chans, LANES), F32),
            pltpu.VMEM((chunks, groups, WIN, chans), BF16),
            pltpu.VMEM((chunks, groups, WIN, chans), BF16),
            pltpu.VMEM((chunks, groups, WIN, chans), BF16),
            pltpu.VMEM((groups, chunks, WIN, chans), BF16),
            pltpu.VMEM((8, LANES), jnp.int32),
            pltpu.VMEM((groups, 8, LANES), jnp.int32),
            pltpu.VMEM((tiles, 8, LANES), F32),
            pltpu.VMEM((tiles, 8, LANES), F32),
            pltpu.VMEM((tiles, CAP * 3 // 2, LANES), BF16),
            pltpu.VMEM((tiles, CAP * 3 // 2, LANES), BF16),
            dma, dma, dma, dma, dma, dma((chunks,)), dma, dma((chunks,)), dma, dma,
            pltpu.SemaphoreType.REGULAR((tiles.bit_length() - 1,)),
            pltpu.VMEM((chans, slots), BF16),
            dma,
        ],
        compiler_params=pltpu.CompilerParams(collective_id=0, has_side_effects=True),
    )(
        node_count, *inputs
    )
    feat, sums = pl.pallas_call(
        finish,
        out_shape=(
            jax.ShapeDtypeStruct((chans, slots), F32),
            jax.ShapeDtypeStruct((chans, VOX_DEV), F32),
        ),
        in_specs=[vmem, vmem],
        out_specs=(vmem, vmem),
    )(feat, sums)
    return feat.T, sums.T


def solution(mesh):
    in_specs = (
        P(("grp", "tile"), None),
        P(("grp", "tile")),
        P(("grp", "tile")),
        P(),
        P(),
        P(),
        P(),
        P(),
        P(),
        P(),
        P(),
        P(),
        P(),
        P(("grp", "tile")),
        P(("grp", "tile"), None),
        P(("grp", "tile")),
    )
    out_specs = (P(("grp", "tile"), None), P(("grp", "tile"), None))
    return jax.shard_map(body, mesh=mesh, in_specs=in_specs, out_specs=out_specs, check_vma=False)
```

```python
import functools
import jax
import jax.numpy as jnp
from jax import lax
from jax.experimental import pallas as pl
from jax.experimental.pallas import tpu as pltpu
from jax.sharding import PartitionSpec as P

HEADS = 12
WIN = 32
VOX_DEV = 256
CAP = 32
LANES = 128
F32 = jnp.float32
BF16 = jnp.bfloat16
NT = (((1,), (1,)), ((), ()))
TN = (((0,), (0,)), ((), ()))
MESH = pl.DeviceIdType.MESH
LOG2E = 1.4426950408889634
INPUTS = 15
FIRST = (0, 1, 2, 4, 5, 3)
LATER = (7, 8, 6, 9, 10, 11, 13, 14, 12)


ROWS = 4
PIECE = 48
UNROLL = 2
UNROLL_TWO = 1


def by_distance(n):
    return sorted(range(n), key=lambda d: (-min(d, n - d), d))


def iota(shape, dim):
    return lax.broadcasted_iota(jnp.int32, shape, dim)


def mm(a, b, dims=(((1,), (0,)), ((), ()))):
    return lax.dot_general(a, b, dims, preferred_element_type=F32)


def normed(x, gain):
    mean = jnp.mean(x, 0, keepdims=True)
    var = jnp.mean((x - mean) ** 2, 0, keepdims=True)
    return ((x - mean) * lax.rsqrt(var + 1e-05) * jnp.concatenate([gain] * (x.shape[1] // LANES), 1)).astype(BF16)


def attend(x, biases, gain, w_qkv, w_out):
    chans = x.shape[0]
    dim = chans // HEADS
    wins = LANES // WIN
    qkv = mm(w_qkv, normed(x, gain))
    query = (qkv[:chans] * (dim**-0.5 * LOG2E)).astype(BF16)
    keys = qkv[chans : 2 * chans].astype(BF16)
    values = qkv[2 * chans :].astype(BF16)
    lane_win = iota((WIN, LANES), 1) // WIN
    own = [lane_win == w for w in range(wins)]
    own_short = [m[:dim] for m in own]
    zero = jnp.zeros((dim, LANES), BF16)
    pairs = [(half, first) for half in range(len(biases)) for first in range(0, HEADS, 2)]
    scores = {}
    for half, first in pairs:
        lanes = slice(LANES * half, LANES * half + LANES)
        rows = slice(first * dim, first * dim + 2 * dim)
        two = query[rows, lanes]
        blocks = jnp.concatenate(
            [jnp.concatenate([two[:dim], zero], 1), jnp.concatenate([zero, two[dim:]], 1)], 0
        )
        full = mm(keys[rows, lanes], blocks, TN)
        for i in range(2):
            wide = full[:, LANES * i : LANES * i + LANES]
            picked = wide[:WIN]
            for w in range(1, wins):
                picked = jnp.where(own[w], wide[WIN * w : WIN * w + WIN], picked)
            scores[half, first + i] = picked + biases[half]
    probs, totals = {}, {}
    for key, score in scores.items():
        weights = jnp.exp2(score - jnp.max(score, 0, keepdims=True))
        totals[key] = 1.0 / jnp.sum(weights, 0, keepdims=True)
        probs[key] = weights.astype(BF16)
    context = {}
    for half, first in pairs:
        rows = slice(first * dim, first * dim + 2 * dim)
        stacked = jnp.concatenate(
            [values[rows, LANES * half + WIN * w : LANES * half + WIN * w + WIN] for w in range(wins)], 0
        )
        mixed = mm(stacked, jnp.concatenate([probs[half, first], probs[half, first + 1]], 1))
        for i in range(2):
            wide = mixed[:, LANES * i : LANES * i + LANES]
            at = [2 * dim * w + dim * i for w in range(wins)]
            picked = wide[at[0] : at[0] + dim]
            for w in range(1, wins):
                picked = jnp.where(own_short[w], wide[at[w] : at[w] + dim], picked)
            context[half, first + i] = (picked * totals[half, first + i]).astype(BF16)
    merged = jnp.concatenate(
        [jnp.concatenate([context[half, h] for h in range(HEADS)], 0) for half in range(len(biases))], 1
    )
    return x + mm(w_out, merged)


def feed(x, gain, w_up, w_down):
    up = mm(w_up, normed(x, gain))
    inside = up * (0.7978845608028654 + 0.035677408136300125 * up * up)
    hidden = (0.5 * up * (1.0 + jnp.tanh(inside))).astype(BF16)
    return x + mm(w_down, hidden)


def swapped(x, groups):
    half = x.shape[0] // groups // 2
    run = WIN // groups
    parts = x.reshape(groups // 2, 2, groups // 2, 2 * run, x.shape[1])
    low = iota((2 * run, x.shape[1]), 0) < run
    out = []
    for b in range(groups // 2):
        for odd in range(2):
            for a in range(groups // 2):
                first, second = parts[a, 0, b], parts[a, 1, b]
                if odd:
                    out.append(jnp.where(low, pltpu.roll(first, run, 0), second))
                else:
                    out.append(jnp.where(low, first, pltpu.roll(second, run, 0)))
    return jnp.concatenate(out, 0)


def turned(w):
    return w.astype(F32).T.astype(BF16)


def columns(row):
    parts = []
    for t in range(row.shape[1] // LANES):
        piece = row[:, LANES * t : LANES * t + LANES].astype(F32)
        parts.append(jnp.broadcast_to(piece, (LANES, LANES)).T)
    return jnp.concatenate(parts, 0)


def place_positions(start, nodes, ids, pos_weight):
    groups, chunks, win, chans = start.shape
    row = iota((16, chans), 0)
    pick = [pos_weight[a : a + 1, :] for a in range(3)]
    spread = jnp.where(row % 3 == 0, pick[0], jnp.where(row % 3 == 1, pick[1], pick[2]))
    high = spread.astype(BF16).astype(F32)
    middle = (spread - high).astype(BF16).astype(F32)
    low = spread - high - middle
    split = jnp.where(row < 3, high, jnp.where(row < 6, middle, jnp.where(row < 9, low, 0.0))).astype(BF16)
    axes = []
    for axis in range(3):
        total = jnp.zeros(ids.shape, jnp.int32)
        for level in range(6):
            total = total + jnp.bitwise_and(jnp.right_shift(ids, 3 * level + axis), 1) * 2**level
        axes.append(total.astype(F32) / 64.0 - 0.5)
    slim = iota((16, LANES), 0)
    for g in range(groups):
        line = [a[g : g + 1, :] for a in axes]
        coords = jnp.where(slim % 3 == 0, line[0], jnp.where(slim % 3 == 1, line[1], line[2])).astype(BF16)
        moved = nodes[:, LANES * g : LANES * g + LANES].astype(F32) + mm(split, coords, TN)
        start[g] = moved.T.astype(BF16).reshape(chunks, win, chans)


def kernel(
    count_ref, *refs, groups, tiles,
):
    far, (feat_out, vox_out), near = refs[:INPUTS], refs[INPUTS : INPUTS + 2], refs[INPUTS + 2 : 2 * INPUTS + 2]
    (
        nodes, ids, pos_weight, gain_one, qkv_one, out_one, gain_two, qkv_two, out_two,
        gain_three, w_up, w_down, slot_ref, owner_ref, voxel_ref,
    ) = near
    loads = refs[2 * INPUTS + 2]
    (
    start, in_one, proj_one, in_two, proj_two, up_turned, norm_one, norm_two, norm_three,
    sent_one, got_one, sent_two, got_two, count_sent, count_got, vox_sent, vox_got, votes_sent, votes_got,
    count_ss, count_rs, vox_ss, vox_rs, one_ss, one_rs, two_ss, two_rs, vote_ss, vote_rs, known, turned_feat, feat_sem, sums_of,
    ) = refs[2 * INPUTS + 3 :]
    me, tile = lax.axis_index("grp"), lax.axis_index("tile")
    chans, slots = nodes.shape
    chunks = start.shape[1]
    block = chunks * WIN
    run = WIN // groups
    rows = groups * WIN
    count = count_ref[0]
    steps = [2**i for i in range(tiles.bit_length() - 1)]

    def across(step):
        return tile + step - 2 * step * lax.rem(tile // step, 2)

    def grp_peer(d):
        return lax.rem(me + d, groups)

    def tile_peer(d):
        return lax.rem(tile + d, tiles)

    barrier = pltpu.get_barrier_semaphore()
    for d in range(1, groups):
        pl.semaphore_signal(barrier, inc=1, device_id=(grp_peer(d), tile), device_id_type=MESH)
    for step in steps:
        pl.semaphore_signal(barrier, inc=1, device_id=(me, across(step)), device_id_type=MESH)

    for i in FIRST + LATER:
        pltpu.make_async_copy(far[i], near[i], loads.at[i]).start()

    def loaded(which):
        for i in which:
            pltpu.make_async_copy(far[i], near[i], loads.at[i]).wait()

    def tell(i):
        pl.semaphore_signal(known.at[i], inc=1, device_id=(me, across(steps[i])), device_id_type=MESH)

    def told(i):
        pl.semaphore_wait(known.at[i], 1)

    def to_group(d, src, dst, ss, rs):
        pltpu.make_async_remote_copy(
            src_ref=src, dst_ref=dst, send_sem=ss, recv_sem=rs,
            device_id=(grp_peer(d), tile), device_id_type=MESH,
        ).start()

    def to_tile(peer, src, dst, ss, rs):
        pltpu.make_async_remote_copy(
            src_ref=src, dst_ref=dst, send_sem=ss, recv_sem=rs,
            device_id=(me, peer), device_id_type=MESH,
        ).start()

    def settle(ref, sem):
        pltpu.make_async_copy(ref, ref, sem).wait()

    def send_one(c):
        for d in range(1, groups):
            to_group(d, sent_one.at[c, grp_peer(d)], got_one.at[c, me], one_ss, one_rs.at[c])

    others = pl.ds(0, groups - 1)
    rest = pl.ds(0, tiles - 1)

    loaded(FIRST)
    count_sent[...] = jnp.full(count_sent.shape, count, jnp.int32)
    count_got[me] = jnp.full(count_sent.shape, count, jnp.int32)
    place_positions(start, nodes, ids[...], pos_weight[...])
    in_one[...] = turned(qkv_one[...])
    proj_one[...] = turned(out_one[...])
    norm_one[...] = jnp.broadcast_to(gain_one[...], (LANES, chans)).T

    key = iota((WIN, LANES), 0)
    window = iota((WIN, LANES), 1) // WIN

    def stage_one(step, carry):
        here = [step * UNROLL + u for u in range(UNROLL)]
        for c in here:
            x = jnp.concatenate([start[g, c] for g in range(groups)], 0).astype(F32)
            biases = []
            for half in range(rows // LANES):
                slot = (window + half * (LANES // WIN)) * block + c * WIN + key
                kept = jnp.where(slot < count, 1.0, 0.0)
                biases.append((kept - 1.0) * 1000000000.0)
            first = attend(x.T, biases, norm_one[...], in_one[...], proj_one[...])
            sent_one[c] = first.T.astype(BF16).reshape(groups, WIN, chans)

        @pl.when(step == 0)
        def _():
            pl.semaphore_wait(barrier, groups - 1 + len(steps))
            for d in range(1, groups):
                to_group(d, count_sent, count_got.at[me], count_ss, count_rs)
            tell(1)

        for c in here:
            got_one[c, me] = sent_one[c, me]
            send_one(c)
        return carry

    lax.fori_loop(0, chunks // UNROLL, stage_one, 0)
    told(1)
    tell(2)

    loaded(LATER)
    in_two[...] = turned(qkv_two[...])
    proj_two[...] = turned(out_two[...])
    up_turned[...] = turned(w_up[...])
    for norm, gain in ((norm_two, gain_two), (norm_three, gain_three)):
        norm[...] = jnp.broadcast_to(gain[...], (LANES, chans)).T
    votes = owner_ref.shape[1]
    owner = owner_ref[...].astype(F32)
    owner_col = columns(owner)
    earlier, later = iota((votes, LANES), 0), iota((votes, LANES), 1)
    ranks = []
    for t in range(votes // LANES):
        same = jnp.logical_and(owner_col == owner[:, LANES * t : LANES * t + LANES], earlier < later + LANES * t)
        ranks.append(jnp.sum(jnp.where(same, 1.0, 0.0), 0, keepdims=True))
    rank = jnp.concatenate(ranks, 1)
    place = owner * CAP + rank
    named = jnp.where(iota((tiles, votes), 0).astype(F32) == owner, voxel_ref[...].astype(F32), 0.0).astype(BF16)
    lane = iota((votes, LANES), 1)
    ranked = (columns(rank) == (lane % CAP).astype(F32)).astype(BF16)
    table = mm(named, ranked)
    share = LANES // CAP
    table = jnp.where(iota((tiles, LANES), 1) // CAP == lax.rem(tile, share), table, 0.0)
    for t in range(tiles):
        vox_sent[t] = jnp.broadcast_to(table[t : t + 1, :], vox_sent.shape[1:])
    vox_got[tile] = vox_sent[tile]
    told(2)
    tell(3)

    settle(count_got.at[others], count_rs)
    counts = jnp.zeros((WIN, LANES), jnp.int32)
    for g in range(groups):
        counts = jnp.where(key // run == g, count_got[g][:1, :], counts)

    def stage_two(step, carry):
        here = [step * UNROLL_TWO + u for u in range(UNROLL_TWO)]
        for c in here:
            settle(got_one.at[c, others], one_rs.at[c])
        for c in here:
            x = swapped(got_one[c].reshape(rows, chans).astype(F32), groups).T
            biases = []
            for half in range(rows // LANES):
                slot = me * block + c * WIN + (half * (LANES // WIN) + window) * run + key % run
                kept = jnp.where(slot < counts, 1.0, 0.0)
                biases.append((kept - 1.0) * 1000000000.0)
            second = attend(x, biases, norm_two[...], in_two[...], proj_two[...])
            third = feed(second, norm_three[...], up_turned[...], w_down[...])
            sent_two[c] = swapped(third.T, groups).astype(BF16).reshape(groups, WIN, chans)
        for c in here:
            got_two[me, c] = sent_two[c, me]
            for d in range(1, groups):
                to_group(d, sent_two.at[c, grp_peer(d)], got_two.at[me, c], two_ss, two_rs.at[c])

        @pl.when(step == 0)
        def _():
            told(3)
            tell(4)

        @pl.when(step == 1)
        def _():
            told(4)
            for d in range(1, tiles):
                to_tile(tile_peer(d), vox_sent.at[tile_peer(d)], vox_got.at[tile], vox_ss, vox_rs)

        return carry

    lax.fori_loop(0, chunks // UNROLL_TWO, stage_two, 0)

    slot_col = columns(slot_ref[...])

    def pick(c):
        chosen = []
        for t in range(rows // LANES):
            slot = (t * (LANES // WIN) + lane // WIN) * block + c * WIN + lane % WIN
            chosen.append((slot_col == slot.astype(F32)).astype(BF16))
        line = iota((rows, chans), 0)
        kept = line // WIN * block + c * WIN + line % WIN < count
        part = jnp.where(kept, got_two[:, c].reshape(rows, chans).astype(F32), 0.0).astype(BF16)
        return mm(jnp.concatenate(chosen, 1), part)

    settle(vox_got.at[rest], vox_rs)
    vox = iota((VOX_DEV, LANES), 0).astype(F32)
    sums = []
    for a in range(tiles // share):
        mine = vox_got[share * a]
        for u in range(1, share):
            mine = mine + vox_got[share * a + u]
        sums.append((vox == mine[:1, :]).astype(BF16))
    deep = tiles // ROWS
    wide = deep // share
    for q in range(ROWS):
        sums_of[q] = jnp.concatenate(sums[q * wide : (q + 1) * wide], 1)
    picked = None
    for c in range(chunks):
        settle(got_two.at[others, c], two_rs.at[c])
        part = pick(c)
        picked = part if picked is None else picked + part
    picked = picked.astype(BF16)

    here, along = tile // deep, lax.rem(tile, deep)
    line = iota((deep * CAP, votes), 0)
    for y in by_distance(ROWS):
        row = lax.rem(here + y, ROWS)
        packing = ((line + row * deep * CAP).astype(F32) == place).astype(BF16)
        mine = mm(packing, picked).reshape(deep, CAP, chans)
        tail = mine[:, :, LANES:]
        tail = jnp.concatenate([tail[:, : CAP // 2], tail[:, CAP // 2 :]], 2)
        votes_sent[pl.ds(row * deep, deep)] = jnp.concatenate([mine[:, :, :LANES], tail], 1).astype(BF16)
        for z in by_distance(deep):
            if y or z:
                peer = row * deep + lax.rem(along + z, deep)
                to_tile(peer, votes_sent.at[peer], votes_got.at[tile], vote_ss, vote_rs.at[y])
    votes_got[tile] = votes_sent[tile]

    short = chans - LANES
    back = got_two[...].reshape(slots, chans)
    feat = jnp.where(iota((slots, chans), 0) < count, back.astype(F32), 0.0)
    turned_feat[...] = feat.T.astype(BF16)
    leave = pltpu.make_async_copy(turned_feat, feat_out, feat_sem)
    leave.start()
    settle(count_got.at[others], count_ss)
    settle(got_one.at[:, others], one_ss)
    settle(got_two.at[others, :], two_ss)
    settle(vox_got.at[rest], vox_ss)
    settle(votes_got.at[rest], vote_ss)
    leave.wait()

    total = None
    for y in by_distance(ROWS):
        row = lax.rem(here + ROWS - y, ROWS)
        settle(votes_got.at[pl.ds(0, deep if y else deep - 1)], vote_rs.at[y])
        got = votes_got[pl.ds(row * deep, deep)]
        head = got[:, :CAP, :].reshape(deep * CAP, LANES)
        tail = got[:, CAP:, :].astype(F32)
        tail = jnp.concatenate([tail[:, :, :short], tail[:, :, short:]], 1).reshape(deep * CAP, short).astype(BF16)
        part = mm(sums_of[row], jnp.concatenate([head, tail], 1))
        total = part if total is None else total + part
    vox_out[...] = total.T


def finish(feat, sums, feat_out, sums_out, feat_near, feat_wide, sums_near, loads, stores):
    pieces = [pl.ds(i * PIECE, PIECE) for i in range(feat.shape[0] // PIECE)]
    last = len(pieces)
    ins = [pltpu.make_async_copy(feat.at[p], feat_near.at[p], loads.at[i]) for i, p in enumerate(pieces)]
    ins.append(pltpu.make_async_copy(sums, sums_near, loads.at[last]))
    outs = [pltpu.make_async_copy(feat_wide.at[p], feat_out.at[p], stores.at[i]) for i, p in enumerate(pieces)]
    outs.append(pltpu.make_async_copy(sums_near, sums_out, stores.at[last]))
    for copy in ins:
        copy.start()
    for i, p in enumerate(pieces):
        ins[i].wait()
        feat_wide[p] = feat_near[p].astype(F32)
        outs[i].start()
    ins[last].wait()
    outs[last].start()
    for copy in outs:
        copy.wait()


def body(
    nodes, node_ids, node_count, pos_weight, gain_one, qkv_one, out_one, gain_two, qkv_two, out_two,
    gain_three, w_up, w_down, vote_slot, vote_owner, vote_voxel,
):
    slots, chans = nodes.shape
    votes = vote_slot.shape[0]
    groups, tiles = lax.axis_size("grp"), lax.axis_size("tile")
    chunks = slots // groups // WIN
    vmem = pl.BlockSpec(memory_space=pltpu.VMEM)
    hbm = pl.BlockSpec(memory_space=pltpu.HBM)
    inputs = (
        nodes.T, node_ids.reshape(slots // LANES, LANES), pos_weight,
        gain_one.reshape(1, chans), qkv_one, out_one, gain_two.reshape(1, chans), qkv_two, out_two,
        gain_three.reshape(1, chans), w_up, w_down.T,
        vote_slot.reshape(1, votes), vote_owner.reshape(1, votes), vote_voxel.reshape(1, votes),
    )
    dma = pltpu.SemaphoreType.DMA


    feat, sums = pl.pallas_call(
        functools.partial(kernel, groups=groups, tiles=tiles),
        out_shape=(
            jax.ShapeDtypeStruct((chans, slots), BF16),
            jax.ShapeDtypeStruct((chans, VOX_DEV), F32),
        ),
        in_specs=[pl.BlockSpec(memory_space=pltpu.SMEM)] + [pl.BlockSpec(memory_space=pltpu.HBM)] * INPUTS,
        out_specs=(pl.BlockSpec(memory_space=pltpu.HBM), vmem),
        scratch_shapes=[pltpu.VMEM(i.shape, i.dtype) for i in inputs]
        + [
            dma((INPUTS,)),
            pltpu.VMEM((groups, chunks, WIN, chans), BF16),
            pltpu.VMEM((3 * chans, chans), BF16),
            pltpu.VMEM((chans, chans), BF16),
            pltpu.VMEM((3 * chans, chans), BF16),
            pltpu.VMEM((chans, chans), BF16),
            pltpu.VMEM((w_up.shape[1], chans), BF16),
            pltpu.VMEM((chans, LANES), F32),
            pltpu.VMEM((chans, LANES), F32),
            pltpu.VMEM((chans, LANES), F32),
            pltpu.VMEM((chunks, groups, WIN, chans), BF16),
            pltpu.VMEM((chunks, groups, WIN, chans), BF16),
            pltpu.VMEM((chunks, groups, WIN, chans), BF16),
            pltpu.VMEM((groups, chunks, WIN, chans), BF16),
            pltpu.VMEM((8, LANES), jnp.int32),
            pltpu.VMEM((groups, 8, LANES), jnp.int32),
            pltpu.VMEM((tiles, 8, LANES), F32),
            pltpu.VMEM((tiles, 8, LANES), F32),
            pltpu.VMEM((tiles, CAP * 3 // 2, LANES), BF16),
            pltpu.VMEM((tiles, CAP * 3 // 2, LANES), BF16),
            dma, dma, dma, dma, dma, dma((chunks,)), dma, dma((chunks,)), dma, dma((ROWS,)),
            pltpu.SemaphoreType.REGULAR((tiles.bit_length() - 1,)),
            pltpu.VMEM((chans, slots), BF16),
            dma,
            pltpu.VMEM((ROWS, VOX_DEV, tiles // ROWS * CAP), BF16),
        ],
        compiler_params=pltpu.CompilerParams(collective_id=0, has_side_effects=True),
    )(
        node_count, *inputs
    )
    feat, sums = pl.pallas_call(
        finish,
        out_shape=(
            jax.ShapeDtypeStruct((chans, slots), F32),
            jax.ShapeDtypeStruct((chans, VOX_DEV), F32),
        ),
        in_specs=[hbm, hbm],
        out_specs=(hbm, hbm),
        scratch_shapes=[
            pltpu.VMEM((chans, slots), BF16),
            pltpu.VMEM((chans, slots), F32),
            pltpu.VMEM((chans, VOX_DEV), F32),
            dma((chans // PIECE + 1,)),
            dma((chans // PIECE + 1,)),
        ],
    )(feat, sums)
    return feat.T, sums.T


def solution(mesh):
    in_specs = (
        P(("grp", "tile"), None),
        P(("grp", "tile")),
        P(("grp", "tile")),
        P(),
        P(),
        P(),
        P(),
        P(),
        P(),
        P(),
        P(),
        P(),
        P(),
        P(("grp", "tile")),
        P(("grp", "tile"), None),
        P(("grp", "tile")),
    )
    out_specs = (P(("grp", "tile"), None), P(("grp", "tile"), None))
    return jax.shard_map(body, mesh=mesh, in_specs=in_specs, out_specs=out_specs, check_vma=False)
```

```python
import functools
import jax
import jax.numpy as jnp
from jax import lax
from jax.experimental import pallas as pl
from jax.experimental.pallas import tpu as pltpu
from jax.sharding import PartitionSpec as P

HEADS = 12
WIN = 32
VOX_DEV = 256
CAP = 32
LANES = 128
F32 = jnp.float32
BF16 = jnp.bfloat16
NT = (((1,), (1,)), ((), ()))
TN = (((0,), (0,)), ((), ()))
MESH = pl.DeviceIdType.MESH
LOG2E = 1.4426950408889634
INPUTS = 15
FIRST = (0, 1, 2, 4, 5, 3)
LATER = (7, 8, 6, 9, 10, 11, 13, 14, 12)


ROWS = 4
PIECE = 48
UNROLL = 2
UNROLL_TWO = 1


def by_distance(n):
    return sorted(range(n), key=lambda d: (-min(d, n - d), d))


def iota(shape, dim):
    return lax.broadcasted_iota(jnp.int32, shape, dim)


def mm(a, b, dims=(((1,), (0,)), ((), ()))):
    return lax.dot_general(a, b, dims, preferred_element_type=F32)


def normed(x, gain):
    mean = jnp.mean(x, 0, keepdims=True)
    var = jnp.mean((x - mean) ** 2, 0, keepdims=True)
    return ((x - mean) * lax.rsqrt(var + 1e-05) * jnp.concatenate([gain] * (x.shape[1] // LANES), 1)).astype(BF16)


def attend(x, biases, gain, w_qkv, w_out):
    chans = x.shape[0]
    dim = chans // HEADS
    qkv = mm(w_qkv, normed(x, gain))
    query = (qkv[:chans] * (dim**-0.5 * LOG2E)).astype(BF16)
    keys = qkv[chans : 2 * chans].astype(BF16)
    values = qkv[2 * chans :].astype(BF16)
    mid = LANES // 2
    upper = iota((WIN, LANES), 1) >= mid
    odd = iota((WIN, LANES), 1) // WIN % 2 == 1
    none = jnp.zeros((WIN, LANES), BF16)
    short, slim = jnp.zeros((2 * dim, LANES), BF16), none[:dim]
    pairs = [(half, first) for half in range(len(biases)) for first in range(0, HEADS, 2)]
    scores = {}
    for half, first in pairs:
        lanes = slice(LANES * half, LANES * half + LANES)
        blocks, stacked = [], []
        for i in range(2):
            rows = slice((first + i) * dim, (first + i) * dim + dim)
            mine = query[rows, lanes]
            split = jnp.concatenate(
                [jnp.where(upper[:dim], slim, mine), jnp.where(upper[:dim], mine, slim)], 0
            )
            blocks.append(jnp.concatenate([short, split] if i else [split, short], 1))
            stacked += [keys[rows, lanes][:, :mid], keys[rows, lanes][:, mid:]]
        full = mm(jnp.concatenate(stacked, 0), jnp.concatenate(blocks, 0), TN)
        for i in range(2):
            wide = full[:, LANES * i : LANES * i + LANES]
            scores[half, first + i] = jnp.where(odd, wide[WIN:], wide[:WIN]) + biases[half]
    probs, totals = {}, {}
    for key, score in scores.items():
        weights = jnp.exp2(score - jnp.max(score, 0, keepdims=True))
        totals[key] = 1.0 / jnp.sum(weights, 0, keepdims=True)
        weights = weights.astype(BF16)
        probs[key] = jnp.concatenate([jnp.where(odd, none, weights), jnp.where(odd, weights, none)], 0)
    context = {}
    for half, first in pairs:
        lanes = slice(LANES * half, LANES * half + LANES)
        mine = values[first * dim : first * dim + 2 * dim, lanes]
        stacked = jnp.concatenate([mine[:, :mid], mine[:, mid:]], 0)
        mixed = mm(stacked, jnp.concatenate([probs[half, first], probs[half, first + 1]], 1))
        for i in range(2):
            wide = mixed[:, LANES * i : LANES * i + LANES]
            low, high = wide[dim * i : dim * i + dim], wide[dim * (i + 2) : dim * (i + 3)]
            context[half, first + i] = (jnp.where(upper[:dim], high, low) * totals[half, first + i]).astype(BF16)
    merged = jnp.concatenate(
        [jnp.concatenate([context[half, h] for h in range(HEADS)], 0) for half in range(len(biases))], 1
    )
    return x + mm(w_out, merged)


def feed(x, gain, w_up, w_down):
    up = mm(w_up, normed(x, gain))
    inside = up * (0.7978845608028654 + 0.035677408136300125 * up * up)
    hidden = (0.5 * up * (1.0 + jnp.tanh(inside))).astype(BF16)
    return x + mm(w_down, hidden)


def swapped(x, groups):
    half = x.shape[0] // groups // 2
    run = WIN // groups
    parts = x.reshape(groups // 2, 2, groups // 2, 2 * run, x.shape[1])
    low = iota((2 * run, x.shape[1]), 0) < run
    out = []
    for b in range(groups // 2):
        for odd in range(2):
            for a in range(groups // 2):
                first, second = parts[a, 0, b], parts[a, 1, b]
                if odd:
                    out.append(jnp.where(low, pltpu.roll(first, run, 0), second))
                else:
                    out.append(jnp.where(low, first, pltpu.roll(second, run, 0)))
    return jnp.concatenate(out, 0)


def turned(w):
    return w.astype(F32).T.astype(BF16)


def columns(row):
    parts = []
    for t in range(row.shape[1] // LANES):
        piece = row[:, LANES * t : LANES * t + LANES].astype(F32)
        parts.append(jnp.broadcast_to(piece, (LANES, LANES)).T)
    return jnp.concatenate(parts, 0)


def place_positions(start, nodes, ids, pos_weight):
    groups, chunks, win, chans = start.shape
    row = iota((16, chans), 0)
    pick = [pos_weight[a : a + 1, :] for a in range(3)]
    spread = jnp.where(row % 3 == 0, pick[0], jnp.where(row % 3 == 1, pick[1], pick[2]))
    high = spread.astype(BF16).astype(F32)
    middle = (spread - high).astype(BF16).astype(F32)
    low = spread - high - middle
    split = jnp.where(row < 3, high, jnp.where(row < 6, middle, jnp.where(row < 9, low, 0.0))).astype(BF16)
    axes = []
    for axis in range(3):
        total = jnp.zeros(ids.shape, jnp.int32)
        for level in range(6):
            total = total + jnp.bitwise_and(jnp.right_shift(ids, 3 * level + axis), 1) * 2**level
        axes.append(total.astype(F32) / 64.0 - 0.5)
    slim = iota((16, LANES), 0)
    for g in range(groups):
        line = [a[g : g + 1, :] for a in axes]
        coords = jnp.where(slim % 3 == 0, line[0], jnp.where(slim % 3 == 1, line[1], line[2])).astype(BF16)
        moved = nodes[:, LANES * g : LANES * g + LANES].astype(F32) + mm(split, coords, TN)
        start[g] = moved.T.astype(BF16).reshape(chunks, win, chans)


def kernel(
    count_ref, *refs, groups, tiles,
):
    far, (feat_out, vox_out), near = refs[:INPUTS], refs[INPUTS : INPUTS + 2], refs[INPUTS + 2 : 2 * INPUTS + 2]
    (
        nodes, ids, pos_weight, gain_one, qkv_one, out_one, gain_two, qkv_two, out_two,
        gain_three, w_up, w_down, slot_ref, owner_ref, voxel_ref,
    ) = near
    loads = refs[2 * INPUTS + 2]
    (
    start, in_one, proj_one, in_two, proj_two, up_turned, norm_one, norm_two, norm_three,
    sent_one, got_one, sent_two, got_two, count_sent, count_got, vox_sent, vox_got, votes_sent, votes_got,
    count_ss, count_rs, vox_ss, vox_rs, one_ss, one_rs, two_ss, two_rs, vote_ss, vote_rs, known, turned_feat, feat_sem, sums_of,
    ) = refs[2 * INPUTS + 3 :]
    me, tile = lax.axis_index("grp"), lax.axis_index("tile")
    chans, slots = nodes.shape
    chunks = start.shape[1]
    block = chunks * WIN
    run = WIN // groups
    rows = groups * WIN
    count = count_ref[0]
    steps = [2**i for i in range(tiles.bit_length() - 1)]

    def across(step):
        return tile + step - 2 * step * lax.rem(tile // step, 2)

    def grp_peer(d):
        return lax.rem(me + d, groups)

    def tile_peer(d):
        return lax.rem(tile + d, tiles)

    barrier = pltpu.get_barrier_semaphore()
    for d in range(1, groups):
        pl.semaphore_signal(barrier, inc=1, device_id=(grp_peer(d), tile), device_id_type=MESH)
    for step in steps:
        pl.semaphore_signal(barrier, inc=1, device_id=(me, across(step)), device_id_type=MESH)

    for i in FIRST + LATER:
        pltpu.make_async_copy(far[i], near[i], loads.at[i]).start()

    def loaded(which):
        for i in which:
            pltpu.make_async_copy(far[i], near[i], loads.at[i]).wait()

    def tell(i):
        pl.semaphore_signal(known.at[i], inc=1, device_id=(me, across(steps[i])), device_id_type=MESH)

    def told(i):
        pl.semaphore_wait(known.at[i], 1)

    def to_group(d, src, dst, ss, rs):
        pltpu.make_async_remote_copy(
            src_ref=src, dst_ref=dst, send_sem=ss, recv_sem=rs,
            device_id=(grp_peer(d), tile), device_id_type=MESH,
        ).start()

    def to_tile(peer, src, dst, ss, rs):
        pltpu.make_async_remote_copy(
            src_ref=src, dst_ref=dst, send_sem=ss, recv_sem=rs,
            device_id=(me, peer), device_id_type=MESH,
        ).start()

    def settle(ref, sem):
        pltpu.make_async_copy(ref, ref, sem).wait()

    def send_one(step):
        both = pl.ds(step * UNROLL, UNROLL)
        for d in range(1, groups):
            to_group(d, sent_one.at[both, grp_peer(d)], got_one.at[both, me], one_ss, one_rs.at[step])

    others = pl.ds(0, groups - 1)
    rest = pl.ds(0, tiles - 1)

    loaded(FIRST)
    count_sent[...] = jnp.full(count_sent.shape, count, jnp.int32)
    count_got[me] = jnp.full(count_sent.shape, count, jnp.int32)
    place_positions(start, nodes, ids[...], pos_weight[...])
    in_one[...] = turned(qkv_one[...])
    proj_one[...] = turned(out_one[...])
    norm_one[...] = jnp.broadcast_to(gain_one[...], (LANES, chans)).T

    key = iota((WIN, LANES), 0)
    window = iota((WIN, LANES), 1) // WIN

    def stage_one(step, carry):
        here = [step * UNROLL + u for u in range(UNROLL)]
        for c in here:
            x = jnp.concatenate([start[g, c] for g in range(groups)], 0).astype(F32)
            biases = []
            for half in range(rows // LANES):
                slot = (window + half * (LANES // WIN)) * block + c * WIN + key
                kept = jnp.where(slot < count, 1.0, 0.0)
                biases.append((kept - 1.0) * 1000000000.0)
            first = attend(x.T, biases, norm_one[...], in_one[...], proj_one[...])
            sent_one[c] = first.T.astype(BF16).reshape(groups, WIN, chans)

        @pl.when(step == 0)
        def _():
            pl.semaphore_wait(barrier, groups - 1 + len(steps))
            for d in range(1, groups):
                to_group(d, count_sent, count_got.at[me], count_ss, count_rs)
            tell(1)

        for c in here:
            got_one[c, me] = sent_one[c, me]
        send_one(step)
        return carry

    lax.fori_loop(0, chunks // UNROLL, stage_one, 0)
    told(1)
    tell(2)

    loaded(LATER)
    in_two[...] = turned(qkv_two[...])
    proj_two[...] = turned(out_two[...])
    up_turned[...] = turned(w_up[...])
    for norm, gain in ((norm_two, gain_two), (norm_three, gain_three)):
        norm[...] = jnp.broadcast_to(gain[...], (LANES, chans)).T
    told(2)
    tell(3)

    settle(count_got.at[others], count_rs)
    counts = jnp.zeros((WIN, LANES), jnp.int32)
    for g in range(groups):
        counts = jnp.where(key // run == g, count_got[g][:1, :], counts)

    def stage_two(step, carry):
        here = [step * UNROLL_TWO + u for u in range(UNROLL_TWO)]

        @pl.when(lax.rem(step * UNROLL_TWO, UNROLL) == 0)
        def _():
            both = pl.ds(step * UNROLL_TWO, UNROLL)
            settle(got_one.at[both, others], one_rs.at[step * UNROLL_TWO // UNROLL])

        for c in here:
            x = swapped(got_one[c].reshape(rows, chans).astype(F32), groups).T
            biases = []
            for half in range(rows // LANES):
                slot = me * block + c * WIN + (half * (LANES // WIN) + window) * run + key % run
                kept = jnp.where(slot < counts, 1.0, 0.0)
                biases.append((kept - 1.0) * 1000000000.0)
            second = attend(x, biases, norm_two[...], in_two[...], proj_two[...])
            third = feed(second, norm_three[...], up_turned[...], w_down[...])
            sent_two[c] = swapped(third.T, groups).astype(BF16).reshape(groups, WIN, chans)
        for c in here:
            got_two[me, c] = sent_two[c, me]
            for d in range(1, groups):
                to_group(d, sent_two.at[c, grp_peer(d)], got_two.at[me, c], two_ss, two_rs.at[c])

        @pl.when(step == 0)
        def _():
            told(3)
            tell(4)

        return carry

    lax.fori_loop(0, chunks // UNROLL_TWO, stage_two, 0)

    votes = owner_ref.shape[1]
    owner = owner_ref[...].astype(F32)
    owner_col = columns(owner)
    earlier, later = iota((votes, LANES), 0), iota((votes, LANES), 1)
    ranks = []
    for t in range(votes // LANES):
        same = jnp.logical_and(owner_col == owner[:, LANES * t : LANES * t + LANES], earlier < later + LANES * t)
        ranks.append(jnp.sum(jnp.where(same, 1.0, 0.0), 0, keepdims=True))
    rank = jnp.concatenate(ranks, 1)
    place = owner * CAP + rank
    named = jnp.where(iota((tiles, votes), 0).astype(F32) == owner, voxel_ref[...].astype(F32), 0.0).astype(BF16)
    lane = iota((votes, LANES), 1)
    ranked = (columns(rank) == (lane % CAP).astype(F32)).astype(BF16)
    table = mm(named, ranked)
    share = LANES // CAP
    table = jnp.where(iota((tiles, LANES), 1) // CAP == lax.rem(tile, share), table, 0.0)
    for t in range(tiles):
        vox_sent[t] = jnp.broadcast_to(table[t : t + 1, :], vox_sent.shape[1:])
    vox_got[tile] = vox_sent[tile]
    told(4)
    for d in range(1, tiles):
        to_tile(tile_peer(d), vox_sent.at[tile_peer(d)], vox_got.at[tile], vox_ss, vox_rs)
    slot_col = columns(slot_ref[...])

    def pick(c):
        chosen = []
        for t in range(rows // LANES):
            slot = (t * (LANES // WIN) + lane // WIN) * block + c * WIN + lane % WIN
            chosen.append((slot_col == slot.astype(F32)).astype(BF16))
        line = iota((rows, chans), 0)
        kept = line // WIN * block + c * WIN + line % WIN < count
        part = jnp.where(kept, got_two[:, c].reshape(rows, chans).astype(F32), 0.0).astype(BF16)
        return mm(jnp.concatenate(chosen, 1), part)

    picked = None
    for c in range(chunks):
        settle(got_two.at[others, c], two_rs.at[c])
        part = pick(c)
        picked = part if picked is None else picked + part
    picked = picked.astype(BF16)

    deep = tiles // ROWS
    here, along = tile // deep, lax.rem(tile, deep)
    line = iota((deep * CAP, votes), 0)
    for y in by_distance(ROWS):
        row = lax.rem(here + y, ROWS)
        packing = ((line + row * deep * CAP).astype(F32) == place).astype(BF16)
        mine = mm(packing, picked).reshape(deep, CAP, chans)
        tail = mine[:, :, LANES:]
        tail = jnp.concatenate([tail[:, : CAP // 2], tail[:, CAP // 2 :]], 2)
        votes_sent[pl.ds(row * deep, deep)] = jnp.concatenate([mine[:, :, :LANES], tail], 1).astype(BF16)
        for z in by_distance(deep):
            if y or z:
                peer = row * deep + lax.rem(along + z, deep)
                to_tile(peer, votes_sent.at[peer], votes_got.at[tile], vote_ss, vote_rs.at[y])
    votes_got[tile] = votes_sent[tile]

    short = chans - LANES
    back = got_two[...].reshape(slots, chans)
    feat = jnp.where(iota((slots, chans), 0) < count, back.astype(F32), 0.0)
    turned_feat[...] = feat.T.astype(BF16)
    leave = pltpu.make_async_copy(turned_feat, feat_out, feat_sem)
    leave.start()
    settle(vox_got.at[rest], vox_rs)
    vox = iota((VOX_DEV, LANES), 0).astype(F32)
    sums = []
    for a in range(tiles // share):
        mine = vox_got[share * a]
        for u in range(1, share):
            mine = mine + vox_got[share * a + u]
        sums.append((vox == mine[:1, :]).astype(BF16))
    wide = deep // share
    for q in range(ROWS):
        sums_of[q] = jnp.concatenate(sums[q * wide : (q + 1) * wide], 1)
    settle(count_got.at[others], count_ss)
    settle(got_one.at[:, others], one_ss)
    settle(got_two.at[others, :], two_ss)
    settle(vox_got.at[rest], vox_ss)
    settle(votes_got.at[rest], vote_ss)
    leave.wait()

    total = None
    for y in by_distance(ROWS):
        row = lax.rem(here + ROWS - y, ROWS)
        settle(votes_got.at[pl.ds(0, deep if y else deep - 1)], vote_rs.at[y])
        got = votes_got[pl.ds(row * deep, deep)]
        head = got[:, :CAP, :].reshape(deep * CAP, LANES)
        tail = got[:, CAP:, :].astype(F32)
        tail = jnp.concatenate([tail[:, :, :short], tail[:, :, short:]], 1).reshape(deep * CAP, short).astype(BF16)
        part = mm(sums_of[row], jnp.concatenate([head, tail], 1))
        total = part if total is None else total + part
    vox_out[...] = total.T


def finish(feat, sums, feat_out, sums_out, feat_near, feat_wide, sums_near, loads, stores):
    pieces = [pl.ds(i * PIECE, PIECE) for i in range(feat.shape[0] // PIECE)]
    last = len(pieces)
    ins = [pltpu.make_async_copy(feat.at[p], feat_near.at[p], loads.at[i]) for i, p in enumerate(pieces)]
    ins.append(pltpu.make_async_copy(sums, sums_near, loads.at[last]))
    outs = [pltpu.make_async_copy(feat_wide.at[p], feat_out.at[p], stores.at[i]) for i, p in enumerate(pieces)]
    outs.append(pltpu.make_async_copy(sums_near, sums_out, stores.at[last]))
    for copy in ins:
        copy.start()
    for i, p in enumerate(pieces):
        ins[i].wait()
        feat_wide[p] = feat_near[p].astype(F32)
        outs[i].start()
    ins[last].wait()
    outs[last].start()
    for copy in outs:
        copy.wait()


def body(
    nodes, node_ids, node_count, pos_weight, gain_one, qkv_one, out_one, gain_two, qkv_two, out_two,
    gain_three, w_up, w_down, vote_slot, vote_owner, vote_voxel,
):
    slots, chans = nodes.shape
    votes = vote_slot.shape[0]
    groups, tiles = lax.axis_size("grp"), lax.axis_size("tile")
    chunks = slots // groups // WIN
    vmem = pl.BlockSpec(memory_space=pltpu.VMEM)
    hbm = pl.BlockSpec(memory_space=pltpu.HBM)
    inputs = (
        nodes.T, node_ids.reshape(slots // LANES, LANES), pos_weight,
        gain_one.reshape(1, chans), qkv_one, out_one, gain_two.reshape(1, chans), qkv_two, out_two,
        gain_three.reshape(1, chans), w_up, w_down.T,
        vote_slot.reshape(1, votes), vote_owner.reshape(1, votes), vote_voxel.reshape(1, votes),
    )
    dma = pltpu.SemaphoreType.DMA


    feat, sums = pl.pallas_call(
        functools.partial(kernel, groups=groups, tiles=tiles),
        out_shape=(
            jax.ShapeDtypeStruct((chans, slots), BF16),
            jax.ShapeDtypeStruct((chans, VOX_DEV), F32),
        ),
        in_specs=[pl.BlockSpec(memory_space=pltpu.SMEM)] + [pl.BlockSpec(memory_space=pltpu.HBM)] * INPUTS,
        out_specs=(pl.BlockSpec(memory_space=pltpu.HBM), vmem),
        scratch_shapes=[pltpu.VMEM(i.shape, i.dtype) for i in inputs]
        + [
            dma((INPUTS,)),
            pltpu.VMEM((groups, chunks, WIN, chans), BF16),
            pltpu.VMEM((3 * chans, chans), BF16),
            pltpu.VMEM((chans, chans), BF16),
            pltpu.VMEM((3 * chans, chans), BF16),
            pltpu.VMEM((chans, chans), BF16),
            pltpu.VMEM((w_up.shape[1], chans), BF16),
            pltpu.VMEM((chans, LANES), F32),
            pltpu.VMEM((chans, LANES), F32),
            pltpu.VMEM((chans, LANES), F32),
            pltpu.VMEM((chunks, groups, WIN, chans), BF16),
            pltpu.VMEM((chunks, groups, WIN, chans), BF16),
            pltpu.VMEM((chunks, groups, WIN, chans), BF16),
            pltpu.VMEM((groups, chunks, WIN, chans), BF16),
            pltpu.VMEM((8, LANES), jnp.int32),
            pltpu.VMEM((groups, 8, LANES), jnp.int32),
            pltpu.VMEM((tiles, 8, LANES), F32),
            pltpu.VMEM((tiles, 8, LANES), F32),
            pltpu.VMEM((tiles, CAP * 3 // 2, LANES), BF16),
            pltpu.VMEM((tiles, CAP * 3 // 2, LANES), BF16),
            dma, dma, dma, dma, dma, dma((chunks // UNROLL,)), dma, dma((chunks,)), dma, dma((ROWS,)),
            pltpu.SemaphoreType.REGULAR((tiles.bit_length() - 1,)),
            pltpu.VMEM((chans, slots), BF16),
            dma,
            pltpu.VMEM((ROWS, VOX_DEV, tiles // ROWS * CAP), BF16),
        ],
        compiler_params=pltpu.CompilerParams(collective_id=0, has_side_effects=True),
    )(
        node_count, *inputs
    )
    feat, sums = pl.pallas_call(
        finish,
        out_shape=(
            jax.ShapeDtypeStruct((chans, slots), F32),
            jax.ShapeDtypeStruct((chans, VOX_DEV), F32),
        ),
        in_specs=[hbm, hbm],
        out_specs=(hbm, hbm),
        scratch_shapes=[
            pltpu.VMEM((chans, slots), BF16),
            pltpu.VMEM((chans, slots), F32),
            pltpu.VMEM((chans, VOX_DEV), F32),
            dma((chans // PIECE + 1,)),
            dma((chans // PIECE + 1,)),
        ],
    )(feat, sums)
    return feat.T, sums.T


def solution(mesh):
    in_specs = (
        P(("grp", "tile"), None),
        P(("grp", "tile")),
        P(("grp", "tile")),
        P(),
        P(),
        P(),
        P(),
        P(),
        P(),
        P(),
        P(),
        P(),
        P(),
        P(("grp", "tile")),
        P(("grp", "tile"), None),
        P(("grp", "tile")),
    )
    out_specs = (P(("grp", "tile"), None), P(("grp", "tile"), None))
    return jax.shard_map(body, mesh=mesh, in_specs=in_specs, out_specs=out_specs, check_vma=False)
```

```python
import functools
import jax
import jax.numpy as jnp
from jax import lax
from jax.experimental import pallas as pl
from jax.experimental.pallas import tpu as pltpu
from jax.sharding import PartitionSpec as P

HEADS = 12
WIN = 32
VOX_DEV = 256
CAP = 32
LANES = 128
F32 = jnp.float32
BF16 = jnp.bfloat16
NT = (((1,), (1,)), ((), ()))
TN = (((0,), (0,)), ((), ()))
MESH = pl.DeviceIdType.MESH
LOG2E = 1.4426950408889634
INPUTS = 15
FIRST = (0, 1, 2, 4, 5, 3)
LATER = (7, 8, 6, 9, 10, 11, 13, 14, 12)


ROWS = 4
PIECE = 48
UNROLL = 2
UNROLL_TWO = 1


def by_distance(n):
    return sorted(range(n), key=lambda d: (-min(d, n - d), d))


def iota(shape, dim):
    return lax.broadcasted_iota(jnp.int32, shape, dim)


def mm(a, b, dims=(((1,), (0,)), ((), ()))):
    return lax.dot_general(a, b, dims, preferred_element_type=F32)


def normed(x, gain):
    mean = jnp.mean(x, 0, keepdims=True)
    var = jnp.mean((x - mean) ** 2, 0, keepdims=True)
    return ((x - mean) * lax.rsqrt(var + 1e-05) * jnp.concatenate([gain] * (x.shape[1] // LANES), 1)).astype(BF16)


def attend(x, biases, gain, w_qkv, w_out):
    chans = x.shape[0]
    dim = chans // HEADS
    qkv = mm(w_qkv, normed(x, gain))
    query = (qkv[:chans] * (dim**-0.5 * LOG2E)).astype(BF16)
    keys = qkv[chans : 2 * chans].astype(BF16)
    values = qkv[2 * chans :].astype(BF16)
    mid = LANES // 2
    upper = iota((WIN, LANES), 1) >= mid
    odd = iota((WIN, LANES), 1) // WIN % 2 == 1
    none = jnp.zeros((WIN, LANES), BF16)
    short, slim = jnp.zeros((2 * dim, LANES), BF16), none[:dim]
    pairs = [(half, first) for half in range(len(biases)) for first in range(0, HEADS, 2)]
    scores = {}
    for half, first in pairs:
        lanes = slice(LANES * half, LANES * half + LANES)
        blocks, stacked = [], []
        for i in range(2):
            rows = slice((first + i) * dim, (first + i) * dim + dim)
            mine = query[rows, lanes]
            split = jnp.concatenate(
                [jnp.where(upper[:dim], slim, mine), jnp.where(upper[:dim], mine, slim)], 0
            )
            blocks.append(jnp.concatenate([short, split] if i else [split, short], 1))
            stacked += [keys[rows, lanes][:, :mid], keys[rows, lanes][:, mid:]]
        full = mm(jnp.concatenate(stacked, 0), jnp.concatenate(blocks, 0), TN)
        for i in range(2):
            wide = full[:, LANES * i : LANES * i + LANES]
            scores[half, first + i] = jnp.where(odd, wide[WIN:], wide[:WIN]) + biases[half]
    probs, totals = {}, {}
    for key, score in scores.items():
        weights = jnp.exp2(score - jnp.max(score, 0, keepdims=True))
        totals[key] = 1.0 / jnp.sum(weights, 0, keepdims=True)
        weights = weights.astype(BF16)
        probs[key] = jnp.concatenate([jnp.where(odd, none, weights), jnp.where(odd, weights, none)], 0)
    context = {}
    for half, first in pairs:
        lanes = slice(LANES * half, LANES * half + LANES)
        mine = values[first * dim : first * dim + 2 * dim, lanes]
        stacked = jnp.concatenate([mine[:, :mid], mine[:, mid:]], 0)
        mixed = mm(stacked, jnp.concatenate([probs[half, first], probs[half, first + 1]], 1))
        for i in range(2):
            wide = mixed[:, LANES * i : LANES * i + LANES]
            low, high = wide[dim * i : dim * i + dim], wide[dim * (i + 2) : dim * (i + 3)]
            context[half, first + i] = (jnp.where(upper[:dim], high, low) * totals[half, first + i]).astype(BF16)
    merged = jnp.concatenate(
        [jnp.concatenate([context[half, h] for h in range(HEADS)], 0) for half in range(len(biases))], 1
    )
    return x + mm(w_out, merged)


def feed(x, gain, w_up, w_down):
    up = mm(w_up, normed(x, gain))
    inside = up * (0.7978845608028654 + 0.035677408136300125 * up * up)
    hidden = (0.5 * up * (1.0 + jnp.tanh(inside))).astype(BF16)
    return x + mm(w_down, hidden)


def swapped(x, groups):
    half = x.shape[0] // groups // 2
    run = WIN // groups
    parts = x.reshape(groups // 2, 2, groups // 2, 2 * run, x.shape[1])
    low = iota((2 * run, x.shape[1]), 0) < run
    out = []
    for b in range(groups // 2):
        for odd in range(2):
            for a in range(groups // 2):
                first, second = parts[a, 0, b], parts[a, 1, b]
                if odd:
                    out.append(jnp.where(low, pltpu.roll(first, run, 0), second))
                else:
                    out.append(jnp.where(low, first, pltpu.roll(second, run, 0)))
    return jnp.concatenate(out, 0)


def turned(w):
    return w.astype(F32).T.astype(BF16)


def columns(row):
    parts = []
    for t in range(row.shape[1] // LANES):
        piece = row[:, LANES * t : LANES * t + LANES].astype(F32)
        parts.append(jnp.broadcast_to(piece, (LANES, LANES)).T)
    return jnp.concatenate(parts, 0)


def place_positions(start, nodes, ids, pos_weight):
    groups, chunks, win, chans = start.shape
    row = iota((16, chans), 0)
    pick = [pos_weight[a : a + 1, :] for a in range(3)]
    spread = jnp.where(row % 3 == 0, pick[0], jnp.where(row % 3 == 1, pick[1], pick[2]))
    high = spread.astype(BF16).astype(F32)
    middle = (spread - high).astype(BF16).astype(F32)
    low = spread - high - middle
    split = jnp.where(row < 3, high, jnp.where(row < 6, middle, jnp.where(row < 9, low, 0.0))).astype(BF16)
    axes = []
    for axis in range(3):
        total = jnp.zeros(ids.shape, jnp.int32)
        for level in range(6):
            total = total + jnp.bitwise_and(jnp.right_shift(ids, 3 * level + axis), 1) * 2**level
        axes.append(total.astype(F32) / 64.0 - 0.5)
    slim = iota((16, LANES), 0)
    for g in range(groups):
        line = [a[g : g + 1, :] for a in axes]
        coords = jnp.where(slim % 3 == 0, line[0], jnp.where(slim % 3 == 1, line[1], line[2])).astype(BF16)
        moved = nodes[:, LANES * g : LANES * g + LANES].astype(F32) + mm(split, coords, TN)
        start[g] = moved.T.astype(BF16).reshape(chunks, win, chans)


def kernel(
    count_ref, *refs, groups, tiles,
):
    far, (feat_out, vox_out), near = refs[:INPUTS], refs[INPUTS : INPUTS + 2], refs[INPUTS + 2 : 2 * INPUTS + 2]
    (
        nodes, ids, pos_weight, gain_one, qkv_one, out_one, gain_two, qkv_two, out_two,
        gain_three, w_up, w_down, slot_ref, owner_ref, voxel_ref,
    ) = near
    loads = refs[2 * INPUTS + 2]
    (
    start, in_one, proj_one, in_two, proj_two, up_turned, norm_one, norm_two, norm_three,
    sent_one, got_one, sent_two, got_two, count_sent, count_got, vox_sent, vox_got, votes_sent, votes_got,
    count_ss, count_rs, vox_ss, vox_rs, one_ss, one_rs, two_ss, two_rs, vote_ss, vote_rs, known, turned_feat, feat_sem, sums_of,
    ) = refs[2 * INPUTS + 3 :]
    me, tile = lax.axis_index("grp"), lax.axis_index("tile")
    chans, slots = nodes.shape
    chunks = start.shape[1]
    block = chunks * WIN
    run = WIN // groups
    rows = groups * WIN
    count = count_ref[0]
    steps = sorted((2**i for i in range(tiles.bit_length() - 1)), key=lambda n: (n != tiles // 8, n))

    def across(step):
        return tile + step - 2 * step * lax.rem(tile // step, 2)

    def grp_peer(d):
        return lax.rem(me + d, groups)

    def tile_peer(d):
        return lax.rem(tile + d, tiles)

    barrier = pltpu.get_barrier_semaphore()
    for d in range(1, groups):
        pl.semaphore_signal(barrier, inc=1, device_id=(grp_peer(d), tile), device_id_type=MESH)
    for step in steps:
        pl.semaphore_signal(barrier, inc=1, device_id=(me, across(step)), device_id_type=MESH)

    for i in FIRST + LATER:
        pltpu.make_async_copy(far[i], near[i], loads.at[i]).start()

    def loaded(which):
        for i in which:
            pltpu.make_async_copy(far[i], near[i], loads.at[i]).wait()

    def tell(i):
        pl.semaphore_signal(known.at[i], inc=1, device_id=(me, across(steps[i])), device_id_type=MESH)

    def told(i):
        pl.semaphore_wait(known.at[i], 1)

    def to_group(d, src, dst, ss, rs):
        pltpu.make_async_remote_copy(
            src_ref=src, dst_ref=dst, send_sem=ss, recv_sem=rs,
            device_id=(grp_peer(d), tile), device_id_type=MESH,
        ).start()

    def to_tile(peer, src, dst, ss, rs):
        pltpu.make_async_remote_copy(
            src_ref=src, dst_ref=dst, send_sem=ss, recv_sem=rs,
            device_id=(me, peer), device_id_type=MESH,
        ).start()

    def settle(ref, sem):
        pltpu.make_async_copy(ref, ref, sem).wait()

    def send_one(step):
        both = pl.ds(step * UNROLL, UNROLL)
        for d in range(1, groups):
            to_group(d, sent_one.at[both, grp_peer(d)], got_one.at[both, me], one_ss, one_rs.at[step])

    others = pl.ds(0, groups - 1)
    rest = pl.ds(0, tiles - 1)

    loaded(FIRST)
    count_sent[...] = jnp.full(count_sent.shape, count, jnp.int32)
    count_got[me] = jnp.full(count_sent.shape, count, jnp.int32)
    place_positions(start, nodes, ids[...], pos_weight[...])
    in_one[...] = turned(qkv_one[...])
    proj_one[...] = turned(out_one[...])
    norm_one[...] = jnp.broadcast_to(gain_one[...], (LANES, chans)).T

    key = iota((WIN, LANES), 0)
    window = iota((WIN, LANES), 1) // WIN

    def stage_one(step, carry):
        here = [step * UNROLL + u for u in range(UNROLL)]
        for c in here:
            x = jnp.concatenate([start[g, c] for g in range(groups)], 0).astype(F32)
            biases = []
            for half in range(rows // LANES):
                slot = (window + half * (LANES // WIN)) * block + c * WIN + key
                kept = jnp.where(slot < count, 1.0, 0.0)
                biases.append((kept - 1.0) * 1000000000.0)
            first = attend(x.T, biases, norm_one[...], in_one[...], proj_one[...])
            sent_one[c] = first.T.astype(BF16).reshape(groups, WIN, chans)

        @pl.when(step == 0)
        def _():
            pl.semaphore_wait(barrier, groups - 1 + len(steps))
            for d in range(1, groups):
                to_group(d, count_sent, count_got.at[me], count_ss, count_rs)
            tell(1)

        for c in here:
            got_one[c, me] = sent_one[c, me]
        send_one(step)
        return carry

    lax.fori_loop(0, chunks // UNROLL, stage_one, 0)
    told(1)
    tell(2)

    loaded(LATER)
    in_two[...] = turned(qkv_two[...])
    proj_two[...] = turned(out_two[...])
    up_turned[...] = turned(w_up[...])
    for norm, gain in ((norm_two, gain_two), (norm_three, gain_three)):
        norm[...] = jnp.broadcast_to(gain[...], (LANES, chans)).T

    settle(count_got.at[others], count_rs)
    counts = jnp.zeros((WIN, LANES), jnp.int32)
    for g in range(groups):
        counts = jnp.where(key // run == g, count_got[g][:1, :], counts)

    def stage_two(step, carry):
        here = [step * UNROLL_TWO + u for u in range(UNROLL_TWO)]

        @pl.when(lax.rem(step * UNROLL_TWO, UNROLL) == 0)
        def _():
            both = pl.ds(step * UNROLL_TWO, UNROLL)
            settle(got_one.at[both, others], one_rs.at[step * UNROLL_TWO // UNROLL])

        for c in here:
            x = swapped(got_one[c].reshape(rows, chans).astype(F32), groups).T
            biases = []
            for half in range(rows // LANES):
                slot = me * block + c * WIN + (half * (LANES // WIN) + window) * run + key % run
                kept = jnp.where(slot < counts, 1.0, 0.0)
                biases.append((kept - 1.0) * 1000000000.0)
            second = attend(x, biases, norm_two[...], in_two[...], proj_two[...])
            third = feed(second, norm_three[...], up_turned[...], w_down[...])
            sent_two[c] = swapped(third.T, groups).astype(BF16).reshape(groups, WIN, chans)
        for c in here:
            got_two[me, c] = sent_two[c, me]
            for d in range(1, groups):
                to_group(d, sent_two.at[c, grp_peer(d)], got_two.at[me, c], two_ss, two_rs.at[c])

        @pl.when(step == 0)
        def _():
            told(2)
            tell(3)

        @pl.when(step == 1)
        def _():
            told(3)
            tell(4)

        return carry

    lax.fori_loop(0, chunks // UNROLL_TWO, stage_two, 0)

    votes = owner_ref.shape[1]
    owner = owner_ref[...].astype(F32)
    owner_col = columns(owner)
    earlier, later = iota((votes, LANES), 0), iota((votes, LANES), 1)
    ranks = []
    for t in range(votes // LANES):
        same = jnp.logical_and(owner_col == owner[:, LANES * t : LANES * t + LANES], earlier < later + LANES * t)
        ranks.append(jnp.sum(jnp.where(same, 1.0, 0.0), 0, keepdims=True))
    rank = jnp.concatenate(ranks, 1)
    place = owner * CAP + rank
    named = jnp.where(iota((tiles, votes), 0).astype(F32) == owner, voxel_ref[...].astype(F32), 0.0).astype(BF16)
    lane = iota((votes, LANES), 1)
    ranked = (columns(rank) == (lane % CAP).astype(F32)).astype(BF16)
    table = mm(named, ranked)
    share = LANES // CAP
    table = jnp.where(iota((tiles, LANES), 1) // CAP == lax.rem(tile, share), table, 0.0)
    for t in range(tiles):
        vox_sent[t] = table[t : t + 1, :]
    vox_got[tile] = vox_sent[tile]
    told(4)
    for d in range(1, tiles):
        to_tile(tile_peer(d), vox_sent.at[tile_peer(d)], vox_got.at[tile], vox_ss, vox_rs)
    slot_col = columns(slot_ref[...])

    def pick(c):
        chosen = []
        for t in range(rows // LANES):
            slot = (t * (LANES // WIN) + lane // WIN) * block + c * WIN + lane % WIN
            chosen.append((slot_col == slot.astype(F32)).astype(BF16))
        line = iota((rows, chans), 0)
        kept = line // WIN * block + c * WIN + line % WIN < count
        part = jnp.where(kept, got_two[:, c].reshape(rows, chans).astype(F32), 0.0).astype(BF16)
        return mm(jnp.concatenate(chosen, 1), part)

    picked = None
    for c in range(chunks):
        settle(got_two.at[others, c], two_rs.at[c])
        part = pick(c)
        picked = part if picked is None else picked + part
    picked = picked.astype(BF16)

    deep = tiles // ROWS
    here, along = tile // deep, lax.rem(tile, deep)
    line = iota((deep * CAP, votes), 0)
    for y in by_distance(ROWS):
        row = lax.rem(here + y, ROWS)
        packing = ((line + row * deep * CAP).astype(F32) == place).astype(BF16)
        mine = mm(packing, picked).reshape(deep, CAP, chans)
        tail = mine[:, :, LANES:]
        tail = jnp.concatenate([tail[:, : CAP // 2], tail[:, CAP // 2 :]], 2)
        votes_sent[pl.ds(row * deep, deep)] = jnp.concatenate([mine[:, :, :LANES], tail], 1).astype(BF16)
        for z in by_distance(deep):
            if y or z:
                peer = row * deep + lax.rem(along + z, deep)
                to_tile(peer, votes_sent.at[peer], votes_got.at[tile], vote_ss, vote_rs.at[y])
    votes_got[tile] = votes_sent[tile]

    short = chans - LANES
    back = got_two[...].reshape(slots, chans)
    feat = jnp.where(iota((slots, chans), 0) < count, back.astype(F32), 0.0)
    turned_feat[...] = feat.T.astype(BF16)
    leave = pltpu.make_async_copy(turned_feat, feat_out, feat_sem)
    leave.start()
    settle(vox_got.at[rest], vox_rs)
    vox = iota((VOX_DEV, LANES), 0).astype(F32)
    sums = []
    for a in range(tiles // share):
        mine = vox_got[share * a]
        for u in range(1, share):
            mine = mine + vox_got[share * a + u]
        sums.append((vox == mine).astype(BF16))
    wide = deep // share
    for q in range(ROWS):
        sums_of[q] = jnp.concatenate(sums[q * wide : (q + 1) * wide], 1)
    settle(count_got.at[others], count_ss)
    settle(got_one.at[:, others], one_ss)
    settle(got_two.at[others, :], two_ss)
    settle(vox_got.at[rest], vox_ss)
    settle(votes_got.at[rest], vote_ss)
    leave.wait()

    total = None
    for y in by_distance(ROWS):
        row = lax.rem(here + ROWS - y, ROWS)
        settle(votes_got.at[pl.ds(0, deep if y else deep - 1)], vote_rs.at[y])
        got = votes_got[pl.ds(row * deep, deep)]
        head = got[:, :CAP, :].reshape(deep * CAP, LANES)
        tail = got[:, CAP:, :].astype(F32)
        tail = jnp.concatenate([tail[:, :, :short], tail[:, :, short:]], 1).reshape(deep * CAP, short).astype(BF16)
        part = mm(sums_of[row], jnp.concatenate([head, tail], 1))
        total = part if total is None else total + part
    vox_out[...] = total.T


def finish(feat, sums, feat_out, sums_out, feat_near, feat_wide, sums_near, loads, stores):
    pieces = [pl.ds(i * PIECE, PIECE) for i in range(feat.shape[0] // PIECE)]
    last = len(pieces)
    ins = [pltpu.make_async_copy(feat.at[p], feat_near.at[p], loads.at[i]) for i, p in enumerate(pieces)]
    ins.append(pltpu.make_async_copy(sums, sums_near, loads.at[last]))
    outs = [pltpu.make_async_copy(feat_wide.at[p], feat_out.at[p], stores.at[i]) for i, p in enumerate(pieces)]
    outs.append(pltpu.make_async_copy(sums_near, sums_out, stores.at[last]))
    for copy in ins:
        copy.start()
    for i, p in enumerate(pieces):
        ins[i].wait()
        feat_wide[p] = feat_near[p].astype(F32)
        outs[i].start()
    ins[last].wait()
    outs[last].start()
    for copy in outs:
        copy.wait()


def body(
    nodes, node_ids, node_count, pos_weight, gain_one, qkv_one, out_one, gain_two, qkv_two, out_two,
    gain_three, w_up, w_down, vote_slot, vote_owner, vote_voxel,
):
    slots, chans = nodes.shape
    votes = vote_slot.shape[0]
    groups, tiles = lax.axis_size("grp"), lax.axis_size("tile")
    chunks = slots // groups // WIN
    vmem = pl.BlockSpec(memory_space=pltpu.VMEM)
    hbm = pl.BlockSpec(memory_space=pltpu.HBM)
    inputs = (
        nodes.T, node_ids.reshape(slots // LANES, LANES), pos_weight,
        gain_one.reshape(1, chans), qkv_one, out_one, gain_two.reshape(1, chans), qkv_two, out_two,
        gain_three.reshape(1, chans), w_up, w_down.T,
        vote_slot.reshape(1, votes), vote_owner.reshape(1, votes), vote_voxel.reshape(1, votes),
    )
    dma = pltpu.SemaphoreType.DMA


    feat, sums = pl.pallas_call(
        functools.partial(kernel, groups=groups, tiles=tiles),
        out_shape=(
            jax.ShapeDtypeStruct((chans, slots), BF16),
            jax.ShapeDtypeStruct((chans, VOX_DEV), F32),
        ),
        in_specs=[pl.BlockSpec(memory_space=pltpu.SMEM)] + [pl.BlockSpec(memory_space=pltpu.HBM)] * INPUTS,
        out_specs=(pl.BlockSpec(memory_space=pltpu.HBM), vmem),
        scratch_shapes=[pltpu.VMEM(i.shape, i.dtype) for i in inputs]
        + [
            dma((INPUTS,)),
            pltpu.VMEM((groups, chunks, WIN, chans), BF16),
            pltpu.VMEM((3 * chans, chans), BF16),
            pltpu.VMEM((chans, chans), BF16),
            pltpu.VMEM((3 * chans, chans), BF16),
            pltpu.VMEM((chans, chans), BF16),
            pltpu.VMEM((w_up.shape[1], chans), BF16),
            pltpu.VMEM((chans, LANES), F32),
            pltpu.VMEM((chans, LANES), F32),
            pltpu.VMEM((chans, LANES), F32),
            pltpu.VMEM((chunks, groups, WIN, chans), BF16),
            pltpu.VMEM((chunks, groups, WIN, chans), BF16),
            pltpu.VMEM((chunks, groups, WIN, chans), BF16),
            pltpu.VMEM((groups, chunks, WIN, chans), BF16),
            pltpu.VMEM((8, LANES), jnp.int32),
            pltpu.VMEM((groups, 8, LANES), jnp.int32),
            pltpu.VMEM((tiles, 1, LANES), F32),
            pltpu.VMEM((tiles, 1, LANES), F32),
            pltpu.VMEM((tiles, CAP * 3 // 2, LANES), BF16),
            pltpu.VMEM((tiles, CAP * 3 // 2, LANES), BF16),
            dma, dma, dma, dma, dma, dma((chunks // UNROLL,)), dma, dma((chunks,)), dma, dma((ROWS,)),
            pltpu.SemaphoreType.REGULAR((tiles.bit_length() - 1,)),
            pltpu.VMEM((chans, slots), BF16),
            dma,
            pltpu.VMEM((ROWS, VOX_DEV, tiles // ROWS * CAP), BF16),
        ],
        compiler_params=pltpu.CompilerParams(collective_id=0, has_side_effects=True),
    )(
        node_count, *inputs
    )
    feat, sums = pl.pallas_call(
        finish,
        out_shape=(
            jax.ShapeDtypeStruct((chans, slots), F32),
            jax.ShapeDtypeStruct((chans, VOX_DEV), F32),
        ),
        in_specs=[hbm, hbm],
        out_specs=(hbm, hbm),
        scratch_shapes=[
            pltpu.VMEM((chans, slots), BF16),
            pltpu.VMEM((chans, slots), F32),
            pltpu.VMEM((chans, VOX_DEV), F32),
            dma((chans // PIECE + 1,)),
            dma((chans // PIECE + 1,)),
        ],
    )(feat, sums)
    return feat.T, sums.T


def solution(mesh):
    in_specs = (
        P(("grp", "tile"), None),
        P(("grp", "tile")),
        P(("grp", "tile")),
        P(),
        P(),
        P(),
        P(),
        P(),
        P(),
        P(),
        P(),
        P(),
        P(),
        P(("grp", "tile")),
        P(("grp", "tile"), None),
        P(("grp", "tile")),
    )
    out_specs = (P(("grp", "tile"), None), P(("grp", "tile"), None))
    return jax.shard_map(body, mesh=mesh, in_specs=in_specs, out_specs=out_specs, check_vma=False)
```
